512 devices in a mesh: seq: 32 (over z, core), hid: 16 (over x, y).
Axes of the slice: x: 4, y: 4, z: 16, core: 2. Of those that a mesh axis runs over, the one named last changes fastest.
Arguments:
- activations: bfloat16 [16384, 4096], P('seq'), may hold values from -6 to 6
- w_inner: bfloat16 [4096, 4096], P('seq', 'hid'), may hold values from -0.09375 to 0.09375
- w_gate: bfloat16 [4096, 4096], P('seq', 'hid'), may hold values from -0.09375 to 0.09375
- w_groups: bfloat16 [4096, 1024], P('seq'), may hold values from -0.09375 to 0.09375
- w_step: bfloat16 [4096, 64], P('seq'), may hold values from -0.09375 to 0.09375
- w_out: bfloat16 [4096, 4096], P('seq', 'hid'), may hold values from -0.09375 to 0.09375
- conv_inner: float32 [4, 4096], P(None, 'hid'), may hold values from -3 to 3
- conv_groups: float32 [4, 1024], replicated, may hold values from -3 to 3
- step_bias: float32 [64], P('hid'), may hold values from -4 to 0
- decay_log: float32 [64], P('hid'), may hold values from -9 to -1
- skip_gain: float32 [64], P('hid'), may hold values from 0.5 to 1.5
- norm_gain: float32 [4096], P('hid'), may hold values from 0.5 to 1.5
Outputs:
- layer_out: bfloat16 [16384, 4096], P('seq', 'hid')
The draws below stay inside these ranges and needn't reach their ends.
All inputs are finite; a program needn't handle non-finite values.
Results may differ from the reference program's by a relative error of at most 0.02.
Values may be sent and summed in bfloat16 or wider, within the bound.
A program may use at most 64 MiB of HBM per device.

```python
import jax
import jax.numpy as jnp
from jax import lax

D = 4096
HEADS = 64
P_SIZE = 64
N = 128
G = 4
Q = 256
K = 4
INNER = 4096
TOKENS = 16384
N_HID = 16


def block_scale(own_key, extent, pieces, low, high):
    loudness = 1.0
    for dim, shards_of in pieces:
        heights = jax.random.uniform(jax.random.fold_in(jax.random.fold_in(own_key, 6), dim), (shards_of,), jnp.float32, low / len(pieces), high / len(pieces))
        loudness = loudness * jnp.repeat(jnp.exp(heights), extent[dim] // shards_of).reshape((-1,) + (1,) * (len(extent) - 1 - dim))
    return loudness


def normal_values(stream_key, dims, width, limit, pieces=(), dtype=jnp.bfloat16):
    level = block_scale(stream_key, dims, pieces, -0.22, 0.18) if pieces else 1.0
    array = jax.random.normal(stream_key, dims, jnp.float32) * width * level
    return jnp.minimum(jnp.maximum(array, -limit), limit).astype(dtype)


def setup_inputs(seed: int = 0) -> dict:
    key_of = jax.random.split(jax.random.key(seed), 13)
    return {
        "activations": normal_values(key_of[0], (TOKENS, D), 1.0, 6.0, ((0, 32),)),
        "w_inner": normal_values(key_of[1], (D, INNER), D ** -0.5, 0.09375, ((0, 32), (1, 16))),
        "w_gate": normal_values(key_of[2], (D, INNER), D ** -0.5, 0.09375, ((0, 32), (1, 16))),
        "w_groups": normal_values(key_of[3], (D, 2 * G * N), D ** -0.5, 0.09375, ((0, 32),)),
        "w_step": normal_values(key_of[4], (D, HEADS), D ** -0.5, 0.09375, ((0, 32),)),
        "w_out": normal_values(key_of[5], (D, INNER), INNER ** -0.5, 0.09375, ((0, 32), (1, 16))),
        "conv_inner": normal_values(key_of[6], (K, INNER), 0.5, 3.0, ((1, 16),), jnp.float32),
        "conv_groups": normal_values(key_of[7], (K, 2 * G * N), 0.5, 3.0, (), jnp.float32),
        "step_bias": jnp.clip(-4.0 + 4.0 * jax.random.uniform(key_of[8], (HEADS,), jnp.float32) ** block_scale(key_of[8], (HEADS,), ((0, 16),), -0.2, 0.2), -4.0, 0.0),
        "decay_log": jnp.clip(-9.0 + 8.0 * jax.random.uniform(key_of[9], (HEADS,), jnp.float32) ** block_scale(key_of[9], (HEADS,), ((0, 16),), -0.2, 0.2), -9.0, -1.0),
        "skip_gain": jnp.clip(0.5 + 1.0 * jax.random.uniform(key_of[10], (HEADS,), jnp.float32) ** block_scale(key_of[10], (HEADS,), ((0, 16),), -0.2, 0.2), 0.5, 1.5),
        "norm_gain": jnp.clip(1.0 + 0.1 * jax.random.normal(key_of[11], (INNER,), jnp.float32), 0.5, 1.5),
    }


def causal_conv(values, kernel):
    tap_count = kernel.shape[0]
    length = values.shape[0]
    padded = jnp.pad(values.astype(jnp.float32), ((tap_count - 1, 0), (0, 0)))
    summed = jnp.zeros(values.shape, jnp.float32)
    for position in range(tap_count):
        summed = summed + padded[position:position + length] * kernel[position]
    return jax.nn.silu(summed).astype(jnp.bfloat16)

def ssd_reference(inner_conv, groups_conv, step_size, rates):
    token_count = inner_conv.shape[0]
    span_count = token_count // Q
    per_group = HEADS // G
    heads_x = inner_conv.reshape(span_count, Q, HEADS, P_SIZE)
    groups_bc = groups_conv.reshape(span_count, Q, G, 2, N)
    steps_all = step_size.reshape(span_count, Q, HEADS)
    ahead = jnp.arange(Q)[:, None] >= jnp.arange(Q)[None, :]

    def advance(state, inputs):
        block_x, block_bc, block_dt = inputs
        block_x = block_x.astype(jnp.float32)
        b_group = block_bc[:, :, 0].astype(jnp.float32)
        c_group = block_bc[:, :, 1].astype(jnp.float32)
        b_heads = jnp.repeat(b_group, per_group, axis=1)
        c_heads = jnp.repeat(c_group, per_group, axis=1)
        cum_decay = jnp.cumsum(block_dt * rates, axis=0)
        scores = jnp.einsum('tgn,sgn->gts', c_group, b_group)
        scores = jnp.repeat(scores, per_group, axis=0)
        decay_t = cum_decay.T
        gap = jnp.where(ahead[None], decay_t[:, :, None] - decay_t[:, None, :], -1e+30)
        mixing = (scores * jnp.exp(gap) * block_dt.T[:, None, :]).astype(jnp.bfloat16)
        intra = jnp.einsum('hts,shp->thp', mixing.astype(jnp.float32), block_x)
        inter = jnp.einsum('thn,hnp->thp', c_heads, state, precision=lax.Precision.HIGHEST)
        inter = inter * jnp.exp(cum_decay)[:, :, None]
        span_total = cum_decay[-1]
        weights_in = jnp.exp(span_total[None, :] - cum_decay) * block_dt
        weighted = (b_heads * weights_in[:, :, None]).astype(jnp.bfloat16)
        fresh = jnp.einsum('shn,shp->hnp', weighted.astype(jnp.float32), block_x)
        state = jnp.exp(span_total)[:, None, None] * state + fresh
        return (state, intra + inter)
    start_state = jnp.zeros((HEADS, N, P_SIZE), jnp.float32)
    _, outputs = lax.scan(advance, start_state, (heads_x, groups_bc, steps_all))
    return outputs.reshape(token_count, HEADS * P_SIZE)

def reference(activations, w_inner, w_gate, w_groups, w_step, w_out, conv_inner, conv_groups, step_bias, decay_log, skip_gain, norm_gain):
    inner_in = jnp.dot(activations, w_inner, preferred_element_type=jnp.float32).astype(jnp.bfloat16)
    gate_in = jnp.dot(activations, w_gate, preferred_element_type=jnp.float32).astype(jnp.bfloat16)
    groups_in = jnp.dot(activations, w_groups, preferred_element_type=jnp.float32).astype(jnp.bfloat16)
    step_raw = jnp.dot(activations, w_step, preferred_element_type=jnp.float32)
    inner_conv = causal_conv(inner_in, conv_inner)
    groups_conv = causal_conv(groups_in, conv_groups)
    step_size = jax.nn.softplus(step_raw + step_bias)
    rates = -jnp.exp(decay_log)
    mixed = ssd_reference(inner_conv, groups_conv, step_size, rates)
    mixed = mixed + jnp.repeat(skip_gain, P_SIZE) * inner_conv.astype(jnp.float32)
    gated = mixed * jax.nn.silu(gate_in.astype(jnp.float32))
    mean_square = lax.optimization_barrier(jnp.mean(gated * gated, axis=1, keepdims=True))
    normed = (gated * lax.rsqrt(mean_square + 1e-05) * norm_gain).astype(jnp.bfloat16)
    block_width = INNER // N_HID
    summed = jnp.zeros((activations.shape[0], D), jnp.float32)
    for block in range(N_HID):
        lower = block * block_width
        partial_out = lax.dot_general(normed[:, lower:lower + block_width], w_out[:, lower:lower + block_width], (((1,), (1,)), ((), ())), preferred_element_type=jnp.float32)
        summed = summed + lax.optimization_barrier(partial_out.astype(jnp.bfloat16)).astype(jnp.float32)
    return summed.astype(jnp.bfloat16)
```

```python
import jax
import jax.numpy as jnp
from jax import lax
from jax.experimental import pallas as pl
from jax.experimental.pallas import tpu as pltpu
from jax.sharding import PartitionSpec as P

F32 = jnp.float32
BF16 = jnp.bfloat16
MESH = pl.DeviceIdType.MESH
INNER = 4096
TOK = 512
HALO = 16
NZ = 16
FAR = ((8, 7), (8, 7), (7, 8), (8, 7), (7, 8), (8, 7), (7, 8))


def remote(src, dst, send, recv, device):
    return pltpu.make_async_remote_copy(
        src_ref=src, dst_ref=dst, send_sem=send, recv_sem=recv, device_id=device, device_id_type=MESH
    )


def split(value):
    high = value.astype(BF16)
    return high, (value - high.astype(F32)).astype(BF16)


def kernel(
    act_hbm,
    wi_hbm,
    wg_hbm,
    wo_ref,
    wgr_ref,
    wst_ref,
    tapi_ref,
    tapg_ref,
    bias_ref,
    decay_ref,
    skip_ref,
    gain_ref,
    out_ref,
    act,
    w_in,
    w_gate,
    w_gs,
    land,
    w_out,
    gath,
    acc_i,
    acc_g,
    acc_s,
    bct,
    xc,
    cols,
    e_own,
    e_sib,
    tbuf,
    pbuf,
    psib,
    local_sem,
    halo_sem,
    zs,
    zr,
    bs,
    br,
    a_s,
    a_r,
    a_l,
    ws,
    wr,
    ys,
    yr,
    es,
    ts,
    tr,
    g1s,
    g1r,
    g2s,
    g2r,
):
    s = lax.axis_index("seq")
    h = lax.axis_index("hid")
    z = s // 2
    c = s % 2
    x = h // 4
    y = h % 4

    def dev(zz, cc, hh):
        return {"seq": 2 * zz + cc, "hid": hh}

    def zmod(v):
        return lax.rem(v + 2 * NZ, NZ)

    def hid_at(dx, dy):
        return lax.rem(x + dx + 4, 4) * 4 + lax.rem(y + dy + 4, 4)

    sib = dev(z, 1 - c, h)
    after = {"seq": lax.rem(s + 1, 32), "hid": h}
    extra = {"seq": lax.rem(s + 2 * c - 1 + 32, 32), "hid": h}

    load_act = pltpu.make_async_copy(act_hbm, act.at[pl.ds(HALO, TOK), :], local_sem.at[0])
    own_rows = pl.ds(pl.multiple_of(s * 128, 128), 128)
    load_in = pltpu.make_async_copy(wi_hbm, w_in.at[own_rows, :], local_sem.at[1])
    load_gate = pltpu.make_async_copy(wg_hbm, w_gate.at[own_rows, :], local_sem.at[2])
    load_in.start()
    load_gate.start()
    load_act.start()

    barrier = pltpu.get_barrier_semaphore()
    for step in (1, -1, 2, -2):
        pl.semaphore_signal(barrier, inc=1, device_id=dev(zmod(z + step), c, h), device_id_type=MESH)
    pl.semaphore_signal(barrier, inc=1, device_id=sib, device_id_type=MESH)
    pl.semaphore_signal(barrier, inc=1, device_id=extra, device_id_type=MESH)
    for step in range(1, 16):
        pl.semaphore_signal(
            barrier, inc=1, device_id=dev(z, c, lax.rem(h + step, 16)), device_id_type=MESH
        )

    tile = wgr_ref[:, pl.ds(pl.multiple_of(x * 256 + (y // 2) * 128, 128), 128)].astype(F32).T
    half = jnp.where(y % 2 == 0, tile[:64], tile[64:])
    steps_t = jnp.concatenate([wst_ref[...].astype(F32)] * 2, axis=1).T
    mine = jnp.where(
        x < 2,
        jnp.where(x == 0, steps_t[0:16], steps_t[16:32]),
        jnp.where(x == 2, steps_t[32:48], steps_t[48:64]),
    )
    own_lanes = pl.ds(pl.multiple_of(s * 128, 128), 128)
    w_gs[0:64, own_lanes] = half.astype(BF16)
    w_gs[64:80, own_lanes] = mine.astype(BF16)
    land[z] = (wo_ref[...].astype(F32) * gain_ref[...]).astype(BF16)

    pl.semaphore_wait(barrier, 21)

    send_halo = remote(
        act_hbm.at[pl.ds(TOK - HALO, HALO), :],
        act.at[pl.ds(0, HALO), :],
        halo_sem.at[0],
        halo_sem.at[1],
        after,
    )

    def block(p, zz):
        row = pl.multiple_of((2 * zz + c) * 128, 128)
        if p == 0:
            return w_gs.at[:, pl.ds(row, 128)]
        part = 64 * ((p - 1) % 2)
        if p < 3:
            return w_in.at[pl.ds(row + part, 64), :]
        if p < 5:
            return w_gate.at[pl.ds(row + part, 64), :]
        return land.at[zz, pl.ds(part, 64), :]

    def sib_block(p, zz):
        row = pl.multiple_of((2 * zz + 1 - c) * 128, 128)
        if p == 0:
            return w_gs.at[:, pl.ds(row, 128)]
        part = 64 * ((p - 1) % 2)
        if p < 3:
            return w_in.at[pl.ds(row + part, 64), :]
        return w_gate.at[pl.ds(row + part, 64), :]

    def origin(d, k):
        return zmod(z - k) if d == 0 else zmod(z + k)

    def ring(p, d, k, recv_k):
        ref = block(p, origin(d, k))
        target = zmod(z + 1) if d == 0 else zmod(z - 1)
        return remote(ref, ref, zs.at[p, d, k], zr.at[p, d, recv_k], dev(target, c, h))

    def to_sib(p, d, k):
        ref = block(p, origin(d, k))
        return remote(ref, ref, bs.at[p, d, k], br.at[p, d, k], sib)

    def from_sib(p, d, k):
        ref = sib_block(p, origin(d, k))
        remote(ref, ref, bs.at[p, d, k], br.at[p, d, k], sib).wait_recv()

    def to_owner(p, zz):
        a = p - 5
        dst = w_out.at[
            pl.ds(pl.multiple_of(128 * c, 128) + 64 * a, 64), pl.ds(pl.multiple_of(256 * h, 256), 256)
        ]
        return remote(block(p, zz), dst, a_s.at[a, zz], a_r.at[a, h], dev(z, c, zz)), (
            pltpu.make_async_copy(block(p, zz), dst, a_l.at[a])
        )

    def hand_on(p, d, k):
        if p < 5:
            to_sib(p, d, k).start()
        else:
            zz = origin(d, k)
            far, near = to_owner(p, zz)

            @pl.when(zz != h)
            def _():
                far.start()

            @pl.when(zz == h)
            def _():
                near.start()

    def first(p):
        ring(p, 0, 0, 1).start()
        ring(p, 1, 0, 1).start()
        hand_on(p, 0, 0)

    def event(p, d, k, forward):
        ring(p, d, k, k).wait_recv()
        if forward:
            ring(p, d, k, k + 1).start()
        hand_on(p, d, k)

    def dots(zz):
        col = pl.ds(pl.multiple_of(zz * 256, 256), 256)
        a = act[:, col]
        acc_i[...] += jnp.dot(a, w_in[col, :], preferred_element_type=F32)
        acc_s[...] += lax.dot_general(
            a, w_gs[:, col], (((1,), (1,)), ((), ())), preferred_element_type=F32
        )

    def gate_dots(zz):
        col = pl.ds(pl.multiple_of(zz * 256, 256), 256)
        acc_g[...] += jnp.dot(act[HALO:, col], w_gate[col, :], preferred_element_type=F32)

    first(0)
    load_in.wait()
    first(1)
    first(2)
    send_halo.start()
    load_gate.wait()
    first(3)
    load_act.wait()
    send_halo.wait()
    acc_i[...] = jnp.zeros_like(acc_i)
    acc_s[...] = jnp.zeros_like(acc_s)
    acc_g[...] = jnp.zeros_like(acc_g)

    def lead(k, last):
        for p in (0, 1, 2):
            for d in (0, 1):
                event(p, d, k, k < FAR[p][d] if last else True)

    def behind(k):
        for p in (0, 1, 2):
            for d in (0, 1):
                from_sib(p, d, k)
        dots(origin(0, k))
        dots(origin(1, k))

    lead(1, False)
    for p in (0, 1, 2):
        from_sib(p, 0, 0)
    dots(z)

    def body(k, carry):
        lead(k, False)
        for d in (0, 1):
            event(3, d, k - 1, True)
        behind(k - 1)
        return carry

    lax.fori_loop(2, 7, body, 0)
    lead(7, True)
    for d in (0, 1):
        event(3, d, 6, True)
    first(4)
    behind(6)
    first(5)
    first(6)
    for p in (0, 1, 2):
        event(p, 0 if FAR[p][0] == 8 else 1, 8, False)
    event(3, 0, 7, True)
    event(3, 1, 7, False)
    behind(7)
    for p in (0, 1, 2):
        from_sib(p, 0 if FAR[p][0] == 8 else 1, 8)
    dots(zmod(z + 8))

    def serve(k, last=False):
        for p in (4, 5, 6):
            for d in (0, 1):
                if not last:
                    event(p, d, k, True)
                elif k <= FAR[p][d]:
                    event(p, d, k, k < FAR[p][d])

    def gate_behind(k):
        for p in (3, 4):
            for d in (0, 1):
                from_sib(p, d, k)
        gate_dots(origin(0, k))
        gate_dots(origin(1, k))

    not_first = jnp.where(s == 0, 0.0, 1.0).astype(F32)
    lane128 = lax.broadcasted_iota(jnp.int32, (TOK, 128), 1)
    raw = acc_s[HALO:, :]
    acc_s[...] = acc_s[...].astype(BF16).astype(F32)
    acc_s[0:HALO, :] = acc_s[0:HALO, :] * not_first
    tap_tile = tapg_ref[:, pl.ds(pl.multiple_of(x * 256 + (y // 2) * 128, 128), 128)]
    tap_g = jnp.where(y % 2 == 0, tap_tile, pltpu.roll(tap_tile, 64, axis=1))
    conv = jnp.zeros((TOK, 80), F32)
    for position in range(4):
        conv = conv + acc_s[pl.ds(HALO - 3 + position, TOK), :] * tap_g[position : position + 1, :80]
    conv = conv * jax.nn.sigmoid(conv)
    both = jnp.where(lane128[:, :80] < 64, conv, raw)
    both_t = jnp.concatenate([both, jnp.zeros((TOK, 48), F32)], axis=1).T
    own_cols = pl.ds(pl.multiple_of(64 * y, 64), 64)
    bct[own_cols, :] = both_t[0:64].astype(BF16)

    def y_copy(j, where):
        rows = bct.at[pl.ds(pl.multiple_of(64 * where, 64), 64), :]
        return remote(rows, rows, ys.at[j - 1], yr.at[j - 1], dev(z, c, hid_at(0, j)))

    for j in (1, 3, 2):
        y_copy(j, y).start()

    serve(1)
    event(3, 0, 8, False)

    step4 = jnp.where(
        y < 2,
        jnp.where(y == 0, both_t[64:68], both_t[68:72]),
        jnp.where(y == 2, both_t[72:76], both_t[76:80]),
    )
    step8 = jnp.concatenate([step4, step4], axis=0)
    head = lax.broadcasted_iota(jnp.int32, (8, TOK), 0) % 4
    lane = lax.broadcasted_iota(jnp.int32, (8, TOK), 1)

    def per_head(ref):
        return jnp.where(
            head < 2, jnp.where(head == 0, ref[0], ref[1]), jnp.where(head == 2, ref[2], ref[3])
        )

    v = step8 + per_head(bias_ref)
    dt = jnp.maximum(v, 0.0) + jnp.log1p(jnp.exp(-jnp.abs(v)))
    cum = dt * -jnp.exp(per_head(decay_ref))
    for shift in (1, 2, 4, 8, 16, 32, 64, 128):
        cum = cum + jnp.where(lane % 256 >= shift, pltpu.roll(cum, shift, axis=1), 0.0)
    last = jnp.where(lane < 256, cum[:, 255:256], cum[:, 511:512])
    weight = jnp.exp(last - cum) * dt
    stack = jnp.concatenate([cum, weight, jnp.exp(cum), jnp.zeros((104, TOK), F32)], axis=0)
    cols[...] = stack.T

    def expand(q):
        halves = []
        for i in (0, 2):
            lo = jnp.broadcast_to(cols[:, 8 * q + i : 8 * q + i + 1], (TOK, 128))
            hi = jnp.broadcast_to(cols[:, 8 * q + i + 1 : 8 * q + i + 2], (TOK, 128))
            halves.append(jnp.where(lane128 < 64, lo, hi))
        return jnp.concatenate(halves, axis=1)

    acc_i[...] = acc_i[...].astype(BF16).astype(F32)
    acc_i[0:HALO, :] = acc_i[0:HALO, :] * not_first
    conv = jnp.zeros((TOK, 256), F32)
    for position in range(4):
        conv = conv + acc_i[pl.ds(HALO - 3 + position, TOK), :] * tapi_ref[position : position + 1, :]
    conv = conv * jax.nn.sigmoid(conv)
    xc[...] = conv.astype(BF16)

    serve(2)

    head_lane = lax.broadcasted_iota(jnp.int32, (1, 256), 1) // 64
    weighted = (xc[...].astype(F32) * expand(1)).astype(BF16)
    expcum = expand(2)
    decay0 = expcum[255:256]
    decay1 = expcum[511:512]

    for j in (1, 2, 3):
        y_copy(j, lax.rem(y + 4 - j, 4)).wait()

    fresh0 = jnp.dot(bct[0:128, 0:256], weighted[0:256], preferred_element_type=F32)
    fresh1 = jnp.dot(bct[0:128, 256:512], weighted[256:512], preferred_element_type=F32)
    end_own = decay1 * fresh0 + fresh1
    total_own = decay0 * decay1
    th, tl = split(jnp.broadcast_to(total_own, (8, 256)))
    tail = jnp.concatenate([th.astype(F32), tl.astype(F32)], axis=0).astype(BF16)
    e_own[0:128, :] = end_own.astype(BF16)
    e_own[128:144, :] = tail
    swap = remote(e_own, e_sib, es.at[0], es.at[1], sib)
    swap.start()

    serve(3)
    swap.wait()

    end_sib = e_sib[0:128, :].astype(F32)
    total_sib = e_sib[128:129, :].astype(F32) + e_sib[136:137, :].astype(F32)

    def my_half(value):
        return jnp.where(c == 0, value[:, 0:128], value[:, 128:256])

    second_decay = jnp.where(c == 0, total_sib, total_own)
    chip_end = second_decay * jnp.where(c == 0, end_own, end_sib) + jnp.where(
        c == 0, end_sib, end_own
    )
    chip_total = jnp.broadcast_to(my_half(total_own * total_sib), (8, 128))
    th, tl = split(chip_total)
    tbuf[z, 0:128, :] = my_half(chip_end).astype(BF16)
    tbuf[z, 128:144, :] = jnp.concatenate([th.astype(F32), tl.astype(F32)], axis=0).astype(BF16)

    def t_send(d, k, hop):
        ref = tbuf.at[origin(d, k)]
        target = zmod(z + hop) if d == 0 else zmod(z - hop)
        return remote(ref, ref, ts.at[hop - 1, d, k], tr.at[d, k + hop], dev(target, c, h))

    def t_recv(d, k):
        ref = tbuf.at[origin(d, k)]
        remote(ref, ref, ts.at[0, d, k], tr.at[d, k], sib).wait_recv()

    sent = []

    def t_start(d, k, hop):
        t_send(d, k, hop).start()
        sent.append((d, k, hop))

    for hop in (2, 1):
        for d in (0, 1):
            t_start(d, 0, hop)

    row = lax.broadcasted_iota(jnp.int32, (256, 256), 0)
    column = lax.broadcasted_iota(jnp.int32, (256, 256), 1)
    c_mat = bct[128:256, :].astype(F32).T.astype(BF16)
    intra = []

    def span(q):
        tokens = slice(256 * q, 256 * q + 256)
        scores = jnp.dot(c_mat[tokens], bct[0:128, tokens], preferred_element_type=F32)
        scores = jnp.where(row >= column, scores, 0.0)
        total = jnp.zeros((256, 256), F32)
        for i in range(4):
            gap = jnp.minimum(cols[tokens, i : i + 1] - cum[i : i + 1, tokens], 0.0)
            mixing = (scores * jnp.exp(gap) * dt[i : i + 1, tokens]).astype(BF16)
            x_head = jnp.where(head_lane == i, xc[tokens, :].astype(F32), 0.0).astype(BF16)
            total = total + jnp.dot(mixing, x_head, preferred_element_type=F32)
        return total

    mixed0 = span(0)
    for d in (0, 1):
        t_recv(d, 2)
        for hop in (2, 1):
            t_start(d, 2, hop)
    serve(4)
    mixed1 = span(1)
    skip = jnp.where(
        head_lane < 2,
        jnp.where(head_lane == 0, skip_ref[0], skip_ref[1]),
        jnp.where(head_lane == 2, skip_ref[2], skip_ref[3]),
    )
    xf = xc[...].astype(F32)
    mixed0 = mixed0 + skip * xf[0:256]
    mixed1 = mixed1 + skip * xf[256:512]
    for d in (0, 1):
        t_recv(d, 4)
        for hop in (2, 1):
            t_start(d, 4, hop)
    serve(5)
    for p in (3, 4):
        from_sib(p, 0, 0)
    gate_dots(z)
    for k in (1, 2):
        gate_behind(k)
    t_recv(0, 6)
    for hop in (2, 1):
        t_start(0, 6, hop)
    t_recv(1, 6)
    t_start(1, 6, 1)
    serve(6)
    for k in (3, 4):
        gate_behind(k)
    serve(7, True)
    for k in (5, 6):
        gate_behind(k)
    for d, ks in ((0, (1, 3, 5, 7, 8)), (1, (1, 3, 5, 7))):
        for k in ks:
            t_recv(d, k)

    prefix = jnp.zeros((128, 128), F32)
    for k in range(15, 0, -1):
        zz = zmod(z - k)
        decay = tbuf[zz, 128:129, :].astype(F32) + tbuf[zz, 136:137, :].astype(F32)
        joined = decay * prefix + tbuf[zz, 0:128, :].astype(F32)
        prefix = jnp.where(z >= k, joined, prefix)
    pbuf[...] = prefix
    swap2 = remote(pbuf, psib, es.at[2], es.at[3], sib)
    swap2.start()
    serve(8, True)
    gate_behind(7)
    for p in (3, 4):
        from_sib(p, 0 if FAR[p][0] == 8 else 1, 8)
    gate_dots(zmod(z + 8))
    swap2.wait()
    other = psib[...]
    before = jnp.where(
        c == 0,
        jnp.concatenate([prefix, other], axis=1),
        jnp.concatenate([other, prefix], axis=1),
    )
    state0 = jnp.where(c == 0, before, total_sib * before + end_sib)
    state1 = decay0 * state0 + fresh0

    def gated(q, mixed, state):
        tokens = slice(256 * q, 256 * q + 256)
        high, low = split(state)
        inter = jnp.dot(c_mat[tokens], high, preferred_element_type=F32)
        inter = inter + jnp.dot(c_mat[tokens], low, preferred_element_type=F32)
        mixed = mixed + inter * expcum[tokens]
        gate = acc_g[tokens, :].astype(BF16).astype(F32)
        gath[tokens, pl.ds(pl.multiple_of(256 * h, 256), 256)] = (
            mixed * (gate * jax.nn.sigmoid(gate))
        ).astype(BF16)

    gated(0, mixed0, state0)
    gated(1, mixed1, state1)

    def offset(u, a, b):
        return hid_at(a, b) if u < 2 else hid_at(b, a)

    def part(u, a, b):
        return gath.at[
            pl.ds(128 * u, 128), pl.ds(pl.multiple_of(256 * offset(u, a, b), 256), 256)
        ]

    def g1(u, slot, a):
        ref = part(u, a, 0)
        step = (1, -1, 1 if u % 2 == 0 else -1)[slot]
        return remote(ref, ref, g1s.at[u, slot], g1r.at[u, slot], dev(z, c, offset(u, step, 0)))

    SIDE = (0, -1, 1, 2)

    def g2(u, j, slot, b):
        ref = part(u, SIDE[j], b)
        step = (1, -1, 1 if u % 2 == 0 else -1)[slot]
        return remote(ref, ref, g2s.at[u, j, slot], g2r.at[u, j, slot], dev(z, c, offset(u, 0, step)))

    def g2_start(u, j):
        g2(u, j, 0, 0).start()
        g2(u, j, 1, 0).start()

    units = (0, 2, 1, 3)
    for u in units:
        g1(u, 0, 0).start()
        g1(u, 1, 0).start()
    for u in units:
        g2_start(u, 0)

    def own_out(cc, hh):
        return w_out.at[
            pl.ds(pl.multiple_of(128 * cc, 128), 128), pl.ds(pl.multiple_of(256 * hh, 256), 256)
        ]

    def out_to_sib(hh):
        return remote(own_out(c, hh), own_out(c, hh), ws.at[hh], wr.at[hh], sib)

    def take_out(hh, carry):
        for a in (0, 1):
            ref = w_out.at[
                pl.ds(pl.multiple_of(128 * c, 128) + 64 * a, 64),
                pl.ds(pl.multiple_of(256 * hh, 256), 256),
            ]

            @pl.when(hh != h)
            def _():
                remote(ref, ref, a_s.at[a, hh], a_r.at[a, hh], sib).wait_recv()

            @pl.when(hh == h)
            def _():
                pltpu.make_async_copy(ref, ref, a_l.at[a]).wait()

        out_to_sib(hh).start()
        return carry

    lax.fori_loop(0, 16, take_out, 0)

    for u in units:
        g1(u, 0, -1).wait_recv()
        if u % 2 == 0:
            g1(u, 2, -1).start()
        g2_start(u, 1)
        g1(u, 1, 1).wait_recv()
        if u % 2 == 1:
            g1(u, 2, 1).start()
        g2_start(u, 2)
    for u in units:
        g1(u, 2, 2).wait_recv()
        g2_start(u, 3)

    def out_from_sib(hh, carry):
        ref = own_out(1 - c, hh)
        remote(ref, ref, ws.at[hh], wr.at[hh], sib).wait_recv()
        return carry

    for j in range(4):
        for u in units:
            g2(u, j, 0, -1).wait_recv()
            if u % 2 == 0:
                g2(u, j, 2, -1).start()
            g2(u, j, 1, 1).wait_recv()
            if u % 2 == 1:
                g2(u, j, 2, 1).start()

    lax.fori_loop(0, 16, out_from_sib, 0)
    for u in units:
        for j in range(4):
            g2(u, j, 2, 2).wait_recv()
        tokens = slice(128 * u, 128 * u + 128)
        value = lax.dot_general(
            gath[tokens, :], w_out[...], (((1,), (1,)), ((), ())), preferred_element_type=F32
        )

        def square(i, total):
            g = gath[tokens, pl.ds(pl.multiple_of(128 * i, 128), 128)].astype(F32)
            return total + g * g

        squares = lax.fori_loop(0, 32, square, jnp.zeros((128, 128), F32))
        mean = jnp.sum(squares, axis=1, keepdims=True) / INNER
        out_ref[tokens, :] = (value * lax.rsqrt(mean + 1e-5)).astype(BF16)

    for p in range(7):
        for d in (0, 1):

            def drain(k, carry):
                ring(p, d, k, k + 1).wait_send()
                return carry

            lax.fori_loop(0, FAR[p][d], drain, 0)
            if p < 5:

                def drain_sib(k, carry):
                    to_sib(p, d, k).wait_send()
                    return carry

                lax.fori_loop(d, FAR[p][d] + 1, drain_sib, 0)

    def drain_out(zz, carry):
        @pl.when(zz != h)
        def _():
            for p in (5, 6):
                to_owner(p, zz)[0].wait_send()

        out_to_sib(zz).wait_send()
        return carry

    lax.fori_loop(0, 16, drain_out, 0)
    for d, k, hop in sent:
        t_send(d, k, hop).wait_send()
    for u in units:
        g1(u, 0, 0).wait_send()
        g1(u, 1, 0).wait_send()
        g1(u, 2, -1 if u % 2 == 0 else 1).wait_send()
        for j in range(4):
            g2(u, j, 0, 0).wait_send()
            g2(u, j, 1, 0).wait_send()
            g2(u, j, 2, -1 if u % 2 == 0 else 1).wait_send()


def local(
    activations,
    w_inner,
    w_gate,
    w_groups,
    w_step,
    w_out,
    conv_inner,
    conv_groups,
    step_bias,
    decay_log,
    skip_gain,
    norm_gain,
):
    anywhere = pl.BlockSpec(memory_space=pl.ANY)
    vmem = pl.BlockSpec(memory_space=pltpu.VMEM)
    smem = pl.BlockSpec(memory_space=pltpu.SMEM)
    dma = pltpu.SemaphoreType.DMA
    return pl.pallas_call(
        kernel,
        out_shape=jax.ShapeDtypeStruct((TOK, 256), BF16),
        in_specs=[anywhere] * 3 + [vmem] * 5 + [smem] * 3 + [vmem],
        out_specs=vmem,
        scratch_shapes=[
            pltpu.VMEM((HALO + TOK, 4096), BF16),
            pltpu.VMEM((4096, 256), BF16),
            pltpu.VMEM((4096, 256), BF16),
            pltpu.VMEM((80, 4096), BF16),
            pltpu.VMEM((16, 128, 256), BF16),
            pltpu.VMEM((256, 4096), BF16),
            pltpu.VMEM((TOK, 4096), BF16),
            pltpu.VMEM((HALO + TOK, 256), F32),
            pltpu.VMEM((TOK, 256), F32),
            pltpu.VMEM((HALO + TOK, 80), F32),
            pltpu.VMEM((256, TOK), BF16),
            pltpu.VMEM((TOK, 256), BF16),
            pltpu.VMEM((TOK, 128), F32),
            pltpu.VMEM((144, 256), BF16),
            pltpu.VMEM((144, 256), BF16),
            pltpu.VMEM((16, 144, 128), BF16),
            pltpu.VMEM((128, 128), F32),
            pltpu.VMEM((128, 128), F32),
            dma((3,)),
            dma((2,)),
            dma((7, 2, 9)),
            dma((7, 2, 9)),
            dma((5, 2, 9)),
            dma((5, 2, 9)),
            dma((2, 16)),
            dma((2, 16)),
            dma((2,)),
            dma((16,)),
            dma((16,)),
            dma((3,)),
            dma((3,)),
            dma((4,)),
            dma((2, 2, 9)),
            dma((2, 9)),
            dma((4, 3)),
            dma((4, 3)),
            dma((4, 4, 3)),
            dma((4, 4, 3)),
        ],
        compiler_params=pltpu.CompilerParams(
            collective_id=0, has_side_effects=True, vmem_limit_bytes=48 * 1024 * 1024
        ),
    )(
        activations,
        w_inner,
        w_gate,
        w_out,
        w_groups,
        w_step,
        conv_inner,
        conv_groups,
        step_bias,
        decay_log,
        skip_gain,
        norm_gain.reshape(1, 256),
    )


def solution(mesh):
    in_specs = (
        P("seq", None),
        P("seq", "hid"),
        P("seq", "hid"),
        P("seq", None),
        P("seq", None),
        P("seq", "hid"),
        P(None, "hid"),
        P(),
        P("hid"),
        P("hid"),
        P("hid"),
        P("hid"),
    )
    return jax.shard_map(
        local, mesh=mesh, in_specs=in_specs, out_specs=P("seq", "hid"), check_vma=False
    )
```

```python
import jax
import jax.numpy as jnp
from jax import lax
from jax.experimental import pallas as pl
from jax.experimental.pallas import tpu as pltpu
from jax.sharding import PartitionSpec as P

F32 = jnp.float32
BF16 = jnp.bfloat16
MESH = pl.DeviceIdType.MESH
INNER = 4096
TOK = 512
HALO = 8
NZ = 16
FAR = ((8, 7), (8, 7), (7, 8), (8, 7), (7, 8), (8, 7), (7, 8))


def remote(src, dst, send, recv, device):
    return pltpu.make_async_remote_copy(
        src_ref=src, dst_ref=dst, send_sem=send, recv_sem=recv, device_id=device, device_id_type=MESH
    )


def split(value):
    high = value.astype(BF16)
    return high, (value - high.astype(F32)).astype(BF16)


def kernel(
    act_hbm,
    wi_hbm,
    wg_hbm,
    wo_hbm,
    wgr_hbm,
    wst_hbm,
    tapi_hbm,
    tapg_hbm,
    bias_hbm,
    decay_hbm,
    skip_hbm,
    gain_hbm,
    out_ref,
    wo_ref,
    wgr_ref,
    wst_ref,
    tapi_ref,
    tapg_ref,
    bias_ref,
    decay_ref,
    skip_ref,
    gain_ref,
    small_sem,
    act,
    w_in,
    w_gate,
    w_gs,
    land,
    w_out,
    gath,
    sq_own,
    sq_in,
    p_up,
    p_down,
    p_own,
    s_far,
    s_up,
    s_down,
    r_up,
    r_down,
    f_up,
    f_down,
    acc_i,
    acc_g,
    acc_s,
    bct,
    xc,
    cols,
    e_own,
    e_sib,
    tbuf,
    pbuf,
    psib,
    local_sem,
    halo_sem,
    zs,
    zr,
    bs,
    br,
    a_s,
    a_r,
    a_l,
    ws,
    wr,
    ys,
    yr,
    es,
    ts,
    tr,
    gs,
    gr,
    qs,
    qr,
    hs,
    hr,
):
    s = lax.axis_index("seq")
    h = lax.axis_index("hid")
    z = s // 2
    c = s % 2
    x = h // 4
    y = h % 4

    def dev(zz, cc, hh):
        return {"seq": 2 * zz + cc, "hid": hh}

    def zmod(v):
        return lax.rem(v + 2 * NZ, NZ)

    def hid_at(dx, dy):
        return lax.rem(x + dx + 4, 4) * 4 + lax.rem(y + dy + 4, 4)

    sib = dev(z, 1 - c, h)
    after = {"seq": lax.rem(s + 1, 32), "hid": h}
    extra = {"seq": lax.rem(s + 2 * c - 1 + 32, 32), "hid": h}

    load_act = pltpu.make_async_copy(act_hbm, act.at[pl.ds(HALO, TOK), :], local_sem.at[0])
    own_rows = pl.ds(pl.multiple_of(s * 128, 128), 128)
    load_in = pltpu.make_async_copy(wi_hbm, w_in.at[own_rows, :], local_sem.at[1])
    load_gate = pltpu.make_async_copy(wg_hbm, w_gate.at[own_rows, :], local_sem.at[2])
    group_cols = pl.ds(pl.multiple_of(x * 256 + (y // 2) * 128, 128), 128)
    small = [
        pltpu.make_async_copy(src, dst, small_sem.at[i])
        for i, (src, dst) in enumerate(
            (
                (wgr_hbm.at[:, group_cols], wgr_ref),
                (wst_hbm, wst_ref),
                (wo_hbm, wo_ref),
                (gain_hbm, gain_ref),
                (tapi_hbm, tapi_ref),
                (tapg_hbm.at[:, group_cols], tapg_ref),
                (bias_hbm, bias_ref),
                (decay_hbm, decay_ref),
                (skip_hbm, skip_ref),
            )
        )
    ]
    load_in.start()
    for item in small:
        item.start()
    load_gate.start()
    load_act.start()

    barrier = pltpu.get_barrier_semaphore()
    for step in (1, -1, 2, -2):
        pl.semaphore_signal(barrier, inc=1, device_id=dev(zmod(z + step), c, h), device_id_type=MESH)
    pl.semaphore_signal(barrier, inc=1, device_id=sib, device_id_type=MESH)
    pl.semaphore_signal(barrier, inc=1, device_id=extra, device_id_type=MESH)
    for step in (1, 2, 3):
        for hh in (hid_at(step, 0), hid_at(0, step)):
            pl.semaphore_signal(barrier, inc=1, device_id=dev(z, c, hh), device_id_type=MESH)

    for item in small:
        item.wait()
    tile = wgr_ref[...].astype(F32).T
    half = jnp.where(y % 2 == 0, tile[:64], tile[64:])
    steps_t = wst_ref[...].astype(F32)
    mine = jnp.where(
        x < 2,
        jnp.where(x == 0, steps_t[0:16], steps_t[16:32]),
        jnp.where(x == 2, steps_t[32:48], steps_t[48:64]),
    )
    own_lanes = pl.ds(pl.multiple_of(s * 128, 128), 128)
    w_gs[0:64, own_lanes] = half.astype(BF16)
    w_gs[64:80, own_lanes] = mine.astype(BF16)
    land[z] = (wo_ref[...].astype(F32) * gain_ref[...]).astype(BF16)

    pl.semaphore_wait(barrier, 12)

    send_halo = remote(
        act_hbm.at[pl.ds(TOK - HALO, HALO), :],
        act.at[pl.ds(0, HALO), :],
        halo_sem.at[0],
        halo_sem.at[1],
        after,
    )

    def block(p, zz):
        row = pl.multiple_of((2 * zz + c) * 128, 128)
        if p == 0:
            return w_gs.at[:, pl.ds(row, 128)]
        part = 64 * ((p - 1) % 2)
        if p < 3:
            return w_in.at[pl.ds(row + part, 64), :]
        if p < 5:
            return w_gate.at[pl.ds(row + part, 64), :]
        return land.at[zz, pl.ds(part, 64), :]

    def sib_block(p, zz):
        row = pl.multiple_of((2 * zz + 1 - c) * 128, 128)
        if p == 0:
            return w_gs.at[:, pl.ds(row, 128)]
        part = 64 * ((p - 1) % 2)
        if p < 3:
            return w_in.at[pl.ds(row + part, 64), :]
        return w_gate.at[pl.ds(row + part, 64), :]

    def origin(d, k):
        return zmod(z - k) if d == 0 else zmod(z + k)

    def ring(p, d, k, recv_k):
        ref = block(p, origin(d, k))
        target = zmod(z + 1) if d == 0 else zmod(z - 1)
        return remote(ref, ref, zs.at[p, d, k], zr.at[p, d, recv_k], dev(target, c, h))

    def to_sib(p, d, k):
        ref = block(p, origin(d, k))
        return remote(ref, ref, bs.at[p, d, k], br.at[p, d, k], sib)

    def from_sib(p, d, k):
        ref = sib_block(p, origin(d, k))
        remote(ref, ref, bs.at[p, d, k], br.at[p, d, k], sib).wait_recv()

    def out_part(a, quarter, cc, column):
        row = pl.multiple_of(256 * quarter + 128 * cc, 128) + 64 * a
        return w_out.at[pl.ds(row, 64), pl.ds(pl.multiple_of(256 * column, 256), 256)]

    def to_owner(p, zz):
        a = p - 5
        return (
            block(p, zz),
            out_part(a, zz % 4, c, x),
            a_s.at[a, zz],
            a_r.at[a, zz % 4, x],
            dev(z, c, (zz // 4) * 4 + y),
        )

    def hand_on(p, d, k):
        if p < 5:
            to_sib(p, d, k).start()
        else:
            zz = origin(d, k)

            @pl.when(zz // 4 != x)
            def _():
                remote(*to_owner(p, zz)).start()

            @pl.when(zz // 4 == x)
            def _():
                pltpu.make_async_copy(*to_owner(p, zz)[:2], a_l.at[p - 5, zz % 4]).start()

    def first(p):
        ring(p, 0, 0, 1).start()
        ring(p, 1, 0, 1).start()
        hand_on(p, 0, 0)

    def event(p, d, k, forward):
        ring(p, d, k, k).wait_recv()
        if forward:
            ring(p, d, k, k + 1).start()
        hand_on(p, d, k)

    def dots_in(zz):
        col = pl.ds(pl.multiple_of(zz * 256, 256), 256)
        acc_i[...] += jnp.dot(act[:, col], w_in[col, :], preferred_element_type=F32)

    def dots_gs(zz):
        col = pl.ds(pl.multiple_of(zz * 256, 256), 256)
        acc_s[...] += lax.dot_general(
            act[:, col], w_gs[:, col], (((1,), (1,)), ((), ())), preferred_element_type=F32
        )

    def gate_dots(zz):
        col = pl.ds(pl.multiple_of(zz * 256, 256), 256)
        acc_g[...] += jnp.dot(act[HALO:, col], w_gate[col, :], preferred_element_type=F32)

    first(0)
    load_in.wait()
    first(1)
    first(2)
    send_halo.start()
    load_gate.wait()
    first(3)
    first(4)
    acc_i[...] = jnp.zeros_like(acc_i)
    acc_s[...] = jnp.zeros_like(acc_s)
    acc_g[...] = jnp.zeros_like(acc_g)

    def serve(pieces, k):
        for p in pieces:
            for d in (0, 1):
                if k <= FAR[p][d]:
                    event(p, d, k, k < FAR[p][d])

    def use(pieces, dots, k, ways=(0, 1)):
        for d in ways:
            arrived = [p for p in pieces for e in (0, 1) if k <= FAR[p][e] and (e == d or k == 8)]
            if k == 8 and d == 1:
                continue
            for p in arrived:
                from_sib(p, d if k < 8 else (0 if FAR[p][0] == 8 else 1), k)
            dots(origin(d, k))

    IN = (1, 2)
    GATE = (3, 4)
    OUT = (5, 6)

    serve((0,), 1)
    serve(IN, 1)
    load_act.wait()
    send_halo.wait()
    for p in (0, 1, 2):
        from_sib(p, 0, 0)
    dots_gs(z)
    dots_in(z)
    for k in (2, 3, 4, 5, 6):
        if k % 2 == 0:
            serve((0,), (2, 5, 8)[k // 2 - 1])
        serve((1,), k)
        use((0,), dots_gs, k - 1)
        if k % 2 == 1:
            serve((0,), (4, 7)[k // 2 - 1])
        use(IN, dots_in, k - 1, (0,))
        serve((2,), k)
        use(IN, dots_in, k - 1, (1,))
        serve(GATE, k - 1)
        if k in (2, 4):
            serve((0,), (3, 6)[k // 2 - 1])
    use((0,), dots_gs, 6)
    serve((1,), 7)
    use((0,), dots_gs, 7)
    use((0,), dots_gs, 8)
    serve((2,), 7)
    use(IN, dots_in, 6)
    serve(GATE, 6)

    not_first = jnp.where(s == 0, 0.0, 1.0).astype(F32)
    lane128 = lax.broadcasted_iota(jnp.int32, (TOK, 128), 1)
    raw = acc_s[HALO:, :]
    acc_s[...] = acc_s[...].astype(BF16).astype(F32)
    acc_s[0:HALO, :] = acc_s[0:HALO, :] * not_first
    tap_tile = tapg_ref[...]
    tap_g = jnp.where(y % 2 == 0, tap_tile, pltpu.roll(tap_tile, 64, axis=1))
    conv = jnp.zeros((TOK, 80), F32)
    for position in range(4):
        conv = conv + acc_s[pl.ds(HALO - 3 + position, TOK), :] * tap_g[position : position + 1, :80]
    conv = conv * jax.nn.sigmoid(conv)
    both = jnp.where(lane128[:, :80] < 64, conv, raw)
    both_t = jnp.concatenate([both, jnp.zeros((TOK, 48), F32)], axis=1).T
    own_cols = pl.ds(pl.multiple_of(64 * y, 64), 64)
    bct[own_cols, :] = both_t[0:64].astype(BF16)

    def y_copy(j, where):
        rows = bct.at[pl.ds(pl.multiple_of(64 * where, 64), 64), :]
        return remote(rows, rows, ys.at[j - 1], yr.at[j - 1], dev(z, c, hid_at(0, j)))

    for j in (1, 3, 2):
        y_copy(j, y).start()

    first(5)
    first(6)
    serve(IN, 8)
    use(IN, dots_in, 7)
    serve(GATE, 7)

    step4 = jnp.where(
        y < 2,
        jnp.where(y == 0, both_t[64:68], both_t[68:72]),
        jnp.where(y == 2, both_t[72:76], both_t[76:80]),
    )
    step8 = jnp.concatenate([step4, step4], axis=0)
    head = lax.broadcasted_iota(jnp.int32, (8, TOK), 0) % 4
    lane = lax.broadcasted_iota(jnp.int32, (8, TOK), 1)

    def per_head(ref):
        return jnp.where(
            head < 2, jnp.where(head == 0, ref[0], ref[1]), jnp.where(head == 2, ref[2], ref[3])
        )

    v = step8 + per_head(bias_ref)
    dt = jnp.maximum(v, 0.0) + jnp.log1p(jnp.exp(-jnp.abs(v)))
    cum = dt * -jnp.exp(per_head(decay_ref))
    for shift in (1, 2, 4, 8, 16, 32, 64, 128):
        cum = cum + jnp.where(lane % 256 >= shift, pltpu.roll(cum, shift, axis=1), 0.0)
    last = jnp.where(lane < 256, cum[:, 255:256], cum[:, 511:512])
    weight = jnp.exp(last - cum) * dt
    stack = jnp.concatenate([cum, weight, jnp.exp(cum), jnp.zeros((104, TOK), F32)], axis=0)
    cols[...] = stack.T

    def expand(q):
        halves = []
        for i in (0, 2):
            lo = jnp.broadcast_to(cols[:, 8 * q + i : 8 * q + i + 1], (TOK, 128))
            hi = jnp.broadcast_to(cols[:, 8 * q + i + 1 : 8 * q + i + 2], (TOK, 128))
            halves.append(jnp.where(lane128 < 64, lo, hi))
        return jnp.concatenate(halves, axis=1)

    use(IN, dots_in, 8)
    serve(GATE, 8)
    acc_i[...] = acc_i[...].astype(BF16).astype(F32)
    acc_i[0:HALO, :] = acc_i[0:HALO, :] * not_first
    conv = jnp.zeros((TOK, 256), F32)
    for position in range(4):
        conv = conv + acc_i[pl.ds(HALO - 3 + position, TOK), :] * tapi_ref[position : position + 1, :]
    conv = conv * jax.nn.sigmoid(conv)
    xc[...] = conv.astype(BF16)

    head_lane = lax.broadcasted_iota(jnp.int32, (1, 256), 1) // 64
    weighted = (xc[...].astype(F32) * expand(1)).astype(BF16)
    expcum = expand(2)
    decay0 = expcum[255:256]
    decay1 = expcum[511:512]

    for j in (1, 2, 3):
        y_copy(j, lax.rem(y + 4 - j, 4)).wait()

    fresh0 = jnp.dot(bct[0:128, 0:256], weighted[0:256], preferred_element_type=F32)
    fresh1 = jnp.dot(bct[0:128, 256:512], weighted[256:512], preferred_element_type=F32)
    end_own = decay1 * fresh0 + fresh1
    total_own = decay0 * decay1
    th, tl = split(jnp.broadcast_to(total_own, (8, 256)))
    tail = jnp.concatenate([th.astype(F32), tl.astype(F32)], axis=0).astype(BF16)
    e_own[0:128, :] = end_own.astype(BF16)
    e_own[128:144, :] = tail
    swap = remote(e_own, e_sib, es.at[0], es.at[1], sib)
    swap.start()

    serve(OUT, 1)
    swap.wait()

    end_sib = e_sib[0:128, :].astype(F32)
    total_sib = e_sib[128:129, :].astype(F32) + e_sib[136:137, :].astype(F32)

    def my_half(value):
        return jnp.where(c == 0, value[:, 0:128], value[:, 128:256])

    second_decay = jnp.where(c == 0, total_sib, total_own)
    chip_end = second_decay * jnp.where(c == 0, end_own, end_sib) + jnp.where(
        c == 0, end_sib, end_own
    )
    chip_total = jnp.broadcast_to(my_half(total_own * total_sib), (8, 128))
    th, tl = split(chip_total)
    tbuf[z, 0:128, :] = my_half(chip_end).astype(BF16)
    tbuf[z, 128:144, :] = jnp.concatenate([th.astype(F32), tl.astype(F32)], axis=0).astype(BF16)

    def t_send(d, k, hop):
        ref = tbuf.at[origin(d, k)]
        target = zmod(z + hop) if d == 0 else zmod(z - hop)
        return remote(ref, ref, ts.at[hop - 1, d, k], tr.at[d, k + hop], dev(target, c, h))

    def t_recv(d, k):
        ref = tbuf.at[origin(d, k)]
        remote(ref, ref, ts.at[0, d, k], tr.at[d, k], sib).wait_recv()

    sent = []

    def t_start(d, k, hop):
        t_send(d, k, hop).start()
        sent.append((d, k, hop))

    for hop in (2, 1):
        for d in (0, 1):
            t_start(d, 0, hop)

    row = lax.broadcasted_iota(jnp.int32, (256, 256), 0)
    column = lax.broadcasted_iota(jnp.int32, (256, 256), 1)
    c_mat = bct[128:256, :].astype(F32).T.astype(BF16)
    intra = []

    def span(q):
        tokens = slice(256 * q, 256 * q + 256)
        scores = jnp.dot(c_mat[tokens], bct[0:128, tokens], preferred_element_type=F32)
        scores = jnp.where(row >= column, scores, 0.0)
        total = jnp.zeros((256, 256), F32)
        for i in range(4):
            gap = jnp.minimum(cols[tokens, i : i + 1] - cum[i : i + 1, tokens], 0.0)
            mixing = (scores * jnp.exp(gap) * dt[i : i + 1, tokens]).astype(BF16)
            x_head = jnp.where(head_lane == i, xc[tokens, :].astype(F32), 0.0).astype(BF16)
            total = total + jnp.dot(mixing, x_head, preferred_element_type=F32)
        return total

    mixed0 = span(0)
    for d in (0, 1):
        t_recv(d, 2)
        for hop in (2, 1):
            t_start(d, 2, hop)
    serve(OUT, 2)
    mixed1 = span(1)
    skip = jnp.where(
        head_lane < 2,
        jnp.where(head_lane == 0, skip_ref[0], skip_ref[1]),
        jnp.where(head_lane == 2, skip_ref[2], skip_ref[3]),
    )
    xf = xc[...].astype(F32)
    mixed0 = mixed0 + skip * xf[0:256]
    mixed1 = mixed1 + skip * xf[256:512]
    for d in (0, 1):
        t_recv(d, 4)
        for hop in (2, 1):
            t_start(d, 4, hop)
    serve(OUT, 3)
    for p in GATE:
        from_sib(p, 0, 0)
    gate_dots(z)
    for k in (1, 2, 3, 4):
        use(GATE, gate_dots, k)
    t_recv(0, 6)
    for hop in (2, 1):
        t_start(0, 6, hop)
    t_recv(1, 6)
    t_start(1, 6, 1)
    serve(OUT, 4)
    for k in (5, 6, 7, 8):
        use(GATE, gate_dots, k)
    for d, ks in ((0, (1, 3, 5, 7, 8)), (1, (1, 3, 5, 7))):
        for k in ks:
            t_recv(d, k)

    prefix = jnp.zeros((128, 128), F32)
    for k in range(15, 0, -1):
        zz = zmod(z - k)
        decay = tbuf[zz, 128:129, :].astype(F32) + tbuf[zz, 136:137, :].astype(F32)
        joined = decay * prefix + tbuf[zz, 0:128, :].astype(F32)
        prefix = jnp.where(z >= k, joined, prefix)
    pbuf[...] = prefix
    swap2 = remote(pbuf, psib, es.at[2], es.at[3], sib)
    swap2.start()
    serve(OUT, 5)
    swap2.wait()
    other = psib[...]
    before = jnp.where(
        c == 0,
        jnp.concatenate([prefix, other], axis=1),
        jnp.concatenate([other, prefix], axis=1),
    )
    state0 = jnp.where(c == 0, before, total_sib * before + end_sib)
    state1 = decay0 * state0 + fresh0

    def gated(q, mixed, state):
        tokens = slice(256 * q, 256 * q + 256)
        high, low = split(state)
        inter = jnp.dot(c_mat[tokens], high, preferred_element_type=F32)
        inter = inter + jnp.dot(c_mat[tokens], low, preferred_element_type=F32)
        mixed = mixed + inter * expcum[tokens]
        gate = acc_g[tokens, :].astype(BF16).astype(F32)
        gath[tokens, pl.ds(pl.multiple_of(256 * x, 256), 256)] = (
            mixed * (gate * jax.nn.sigmoid(gate))
        ).astype(BF16)

    gated(0, mixed0, state0)
    gated(1, mixed1, state1)

    def part(u, a, first_row, rows):
        column = pl.multiple_of(256 * lax.rem(x + a + 4, 4), 256)
        return gath.at[pl.ds(128 * u + first_row, rows), pl.ds(column, 256)]

    STEP = (1, -1)

    def g_near(u, way, a):
        ref = part(u, a, 0, 128)
        return remote(ref, ref, gs.at[u, way], gr.at[u, way], dev(z, c, hid_at(STEP[way], 0)))

    def g_far(u, way, a):
        ref = part(u, a, 64 * way, 64)
        return remote(
            ref, ref, gs.at[u, 2 + way], gr.at[u, 2 + way], dev(z, c, hid_at(STEP[way], 0))
        )

    for u in range(4):
        for way in (0, 1):
            g_near(u, way, 0).start()

    def out_block(cc, quarter, column):
        return w_out.at[
            pl.ds(pl.multiple_of(256 * quarter + 128 * cc, 128), 128),
            pl.ds(pl.multiple_of(256 * column, 256), 256),
        ]

    def out_to_sib(i):
        ref = out_block(c, i // 4, i % 4)
        return remote(ref, ref, ws.at[i], wr.at[i], sib)

    def take_out(i, carry):
        for a in (0, 1):
            ref = out_part(a, i // 4, c, i % 4)

            @pl.when(i % 4 != x)
            def _():
                remote(ref, ref, a_s.at[a, i], a_r.at[a, i // 4, i % 4], sib).wait_recv()

            @pl.when(i % 4 == x)
            def _():
                pltpu.make_async_copy(ref, ref, a_l.at[a, i // 4]).wait()

        out_to_sib(i).start()
        return carry

    def out_from_sib(i, carry):
        ref = out_block(1 - c, i // 4, i % 4)
        remote(ref, ref, ws.at[i], wr.at[i], sib).wait_recv()
        return carry

    def drain_out(i, carry):
        @pl.when(i // 4 != x)
        def _():
            for p in (5, 6):
                remote(*to_owner(p, i)).wait_send()

        out_to_sib(i).wait_send()
        return carry

    def drain_weights():
        for p in range(7):
            for d in (0, 1):

                def drain(k, carry):
                    ring(p, d, k, k + 1).wait_send()
                    return carry

                lax.fori_loop(0, FAR[p][d], drain, 0)
                if p < 5:

                    def drain_sib(k, carry):
                        to_sib(p, d, k).wait_send()
                        return carry

                    lax.fori_loop(d, FAR[p][d] + 1, drain_sib, 0)

    serve(OUT, 6)
    for u in range(4):
        for way in (0, 1):
            g_near(u, way, -STEP[way]).wait_recv()
            g_far(u, way, -STEP[way]).start()
        if u < 2:
            serve(OUT, 7 + u)
    lax.fori_loop(0, 16, take_out, 0)
    drain_weights()
    lax.fori_loop(0, 16, out_from_sib, 0)

    def product(u, offset):
        rows = pl.ds(pl.multiple_of(256 * lax.rem(y + offset, 4), 256), 256)
        return lax.dot_general(
            gath[128 * u : 128 * u + 128, :],
            w_out[rows, :],
            (((1,), (1,)), ((), ())),
            preferred_element_type=F32,
        )

    def along(u, slot, way, src, dst):
        return remote(
            src, dst, hs.at[u, slot, way], hr.at[u, slot, way], dev(z, c, hid_at(0, STEP[way]))
        )

    top = pl.ds(0, 64)
    low = pl.ds(64, 64)

    def far_send(u, way):
        return along(u, 0, way, s_far.at[u, (top, low)[way]], (r_up, r_down)[way].at[u])

    def early_send(u, way):
        rows = (low, top)[way]
        return along(u, 1, way, (s_up, s_down)[way].at[u, rows], (f_up, f_down)[way].at[u, rows])

    def late_send(u, way):
        rows = (top, low)[way]
        return along(u, 2, way, (s_up, s_down)[way].at[u, rows], (f_up, f_down)[way].at[u, rows])

    def square_send(u, j):
        return remote(
            sq_own.at[u], sq_in.at[u, j - 1], qs.at[u, j - 1], qr.at[u, j - 1], dev(z, c, hid_at(0, j))
        )

    def multiply(u):
        for way in (0, 1):
            g_far(u, way, 2).wait_recv()
        s_far[u] = product(u, 2).astype(BF16)
        for way in (0, 1):
            far_send(u, way).start()
        up = product(u, 1)
        s_up[u, 64:128, :] = up[64:128].astype(BF16)
        p_up[u] = up[0:64]
        down = product(u, 3)
        s_down[u, 0:64, :] = down[0:64].astype(BF16)
        p_down[u] = down[64:128]
        for way in (0, 1):
            early_send(u, way).start()
        total = jnp.zeros((128, 128), F32)
        for i in range(8):
            g = gath[128 * u : 128 * u + 128, 128 * i : 128 * i + 128].astype(F32)
            total = total + g * g
        sq_own[u] = jnp.broadcast_to(jnp.sum(total.T, axis=0, keepdims=True), (8, 128))
        for j in (1, 3, 2):
            square_send(u, j).start()
        p_own[u] = product(u, 0)

    def add(u):
        far_send(u, 0).wait_recv()
        s_up[u, 0:64, :] = (p_up[u] + r_up[u].astype(F32)).astype(BF16)
        late_send(u, 0).start()
        far_send(u, 1).wait_recv()
        s_down[u, 64:128, :] = (p_down[u] + r_down[u].astype(F32)).astype(BF16)
        late_send(u, 1).start()

    def finish(u):
        for way in (0, 1):
            early_send(u, way).wait_recv()
            late_send(u, way).wait_recv()
        for j in (1, 2, 3):
            square_send(u, j).wait_recv()
        squares = sq_own[u] + sq_in[u, 0] + sq_in[u, 1] + sq_in[u, 2]
        scale = lax.rsqrt(squares / INNER + 1e-5)
        scale = jnp.broadcast_to(scale[0:1], (128, 128)).T
        value = p_own[u] + f_up[u].astype(F32) + f_down[u].astype(F32)
        for half_of in (0, 128):
            out_ref[128 * u : 128 * u + 128, half_of : half_of + 128] = (
                value[:, half_of : half_of + 128] * scale
            ).astype(BF16)

    multiply(0)
    multiply(1)
    add(0)
    multiply(2)
    add(1)
    multiply(3)
    add(2)
    finish(0)
    lax.fori_loop(0, 16, drain_out, 0)
    for d, k, hop in sent:
        t_send(d, k, hop).wait_send()
    add(3)
    for u in (1, 2, 3):
        finish(u)
    for u in range(4):
        for way in (0, 1):
            g_near(u, way, 0).wait_send()
            g_far(u, way, -STEP[way]).wait_send()
            far_send(u, way).wait_send()
            early_send(u, way).wait_send()
            late_send(u, way).wait_send()
        for j in (1, 2, 3):
            square_send(u, j).wait_send()


def local(
    activations,
    w_inner,
    w_gate,
    w_groups,
    w_step,
    w_out,
    conv_inner,
    conv_groups,
    step_bias,
    decay_log,
    skip_gain,
    norm_gain,
):
    anywhere = pl.BlockSpec(memory_space=pl.ANY)
    vmem = pl.BlockSpec(memory_space=pltpu.VMEM)
    dma = pltpu.SemaphoreType.DMA
    return pl.pallas_call(
        kernel,
        out_shape=jax.ShapeDtypeStruct((TOK, 256), BF16),
        in_specs=[anywhere] * 12,
        out_specs=vmem,
        scratch_shapes=[
            pltpu.VMEM((128, 256), BF16),
            pltpu.VMEM((128, 128), BF16),
            pltpu.VMEM((64, 128), BF16),
            pltpu.VMEM((4, 256), F32),
            pltpu.VMEM((4, 128), F32),
            pltpu.SMEM((4,), F32),
            pltpu.SMEM((4,), F32),
            pltpu.SMEM((4,), F32),
            pltpu.VMEM((1, 256), F32),
            dma((9,)),
            pltpu.VMEM((HALO + TOK, 4096), BF16),
            pltpu.VMEM((4096, 256), BF16),
            pltpu.VMEM((4096, 256), BF16),
            pltpu.VMEM((80, 4096), BF16),
            pltpu.VMEM((16, 128, 256), BF16),
            pltpu.VMEM((1024, 1024), BF16),
            pltpu.VMEM((TOK, 1024), BF16),
            pltpu.VMEM((4, 8, 128), F32),
            pltpu.VMEM((4, 3, 8, 128), F32),
            pltpu.VMEM((4, 64, 256), F32),
            pltpu.VMEM((4, 64, 256), F32),
            pltpu.VMEM((4, 128, 256), F32),
            pltpu.VMEM((4, 128, 256), BF16),
            pltpu.VMEM((4, 128, 256), BF16),
            pltpu.VMEM((4, 128, 256), BF16),
            pltpu.VMEM((4, 64, 256), BF16),
            pltpu.VMEM((4, 64, 256), BF16),
            pltpu.VMEM((4, 128, 256), BF16),
            pltpu.VMEM((4, 128, 256), BF16),
            pltpu.VMEM((HALO + TOK, 256), F32),
            pltpu.VMEM((TOK, 256), F32),
            pltpu.VMEM((HALO + TOK, 80), F32),
            pltpu.VMEM((256, TOK), BF16),
            pltpu.VMEM((TOK, 256), BF16),
            pltpu.VMEM((TOK, 128), F32),
            pltpu.VMEM((144, 256), BF16),
            pltpu.VMEM((144, 256), BF16),
            pltpu.VMEM((16, 144, 128), BF16),
            pltpu.VMEM((128, 128), F32),
            pltpu.VMEM((128, 128), F32),
            dma((3,)),
            dma((2,)),
            dma((7, 2, 9)),
            dma((7, 2, 9)),
            dma((5, 2, 9)),
            dma((5, 2, 9)),
            dma((2, 16)),
            dma((2, 4, 4)),
            dma((2, 4)),
            dma((16,)),
            dma((16,)),
            dma((3,)),
            dma((3,)),
            dma((4,)),
            dma((2, 2, 9)),
            dma((2, 9)),
            dma((4, 4)),
            dma((4, 4)),
            dma((4, 3)),
            dma((4, 3)),
            dma((4, 3, 2)),
            dma((4, 3, 2)),
        ],
        compiler_params=pltpu.CompilerParams(
            collective_id=0, has_side_effects=True, vmem_limit_bytes=67043328
        ),
    )(
        activations,
        w_inner,
        w_gate,
        w_out,
        w_groups,
        w_step.T,
        conv_inner,
        conv_groups,
        step_bias,
        decay_log,
        skip_gain,
        norm_gain.reshape(1, 256),
    )


def solution(mesh):
    in_specs = (
        P("seq", None),
        P("seq", "hid"),
        P("seq", "hid"),
        P("seq", None),
        P("seq", None),
        P("seq", "hid"),
        P(None, "hid"),
        P(),
        P("hid"),
        P("hid"),
        P("hid"),
        P("hid"),
    )
    return jax.shard_map(
        local, mesh=mesh, in_specs=in_specs, out_specs=P("seq", "hid"), check_vma=False
    )
```

```python
import jax
import jax.numpy as jnp
from jax import lax
from jax.experimental import pallas as pl
from jax.experimental.pallas import tpu as pltpu
from jax.sharding import PartitionSpec as P

F32 = jnp.float32
BF16 = jnp.bfloat16
MESH = pl.DeviceIdType.MESH
INNER = 4096
TOK = 512
HALO = 8
NZ = 16
FAR = ((8, 7), (8, 7), (7, 8), (8, 7), (7, 8))


def remote(src, dst, send, recv, device):
    return pltpu.make_async_remote_copy(
        src_ref=src, dst_ref=dst, send_sem=send, recv_sem=recv, device_id=device, device_id_type=MESH
    )


def split(value):
    high = value.astype(BF16)
    return high, (value - high.astype(F32)).astype(BF16)


def kernel(
    act_hbm,
    wi_hbm,
    wg_hbm,
    wo_hbm,
    wgr_hbm,
    wst_hbm,
    tapi_hbm,
    tapg_hbm,
    bias_hbm,
    decay_hbm,
    skip_hbm,
    gain_hbm,
    out_ref,
    wo_ref,
    wgr_ref,
    wst_ref,
    tapi_ref,
    tapg_ref,
    bias_ref,
    decay_ref,
    skip_ref,
    gain_ref,
    small_sem,
    act,
    w_in,
    w_gate,
    w_gs,
    land,
    w_out,
    gath,
    sq_own,
    sq_in,
    p_up,
    p_down,
    p_own,
    s_far,
    s_up,
    s_down,
    r_up,
    r_down,
    f_up,
    f_down,
    acc_i,
    acc_g,
    acc_s,
    bct,
    xc,
    cols,
    e_own,
    e_sib,
    tbuf,
    pbuf,
    psib,
    local_sem,
    halo_sem,
    zs,
    zr,
    bs,
    br,
    cs,
    cr,
    os_,
    orr,
    ws,
    wr,
    ys,
    yr,
    es,
    ts,
    tr,
    gs,
    gr,
    qs,
    qr,
    hs,
    hr,
):
    s = lax.axis_index("seq")
    h = lax.axis_index("hid")
    z = s // 2
    c = s % 2
    x = h // 4
    y = h % 4

    def dev(zz, cc, hh):
        return {"seq": 2 * zz + cc, "hid": hh}

    def zmod(v):
        return lax.rem(v + 2 * NZ, NZ)

    def hid_at(dx, dy):
        return lax.rem(x + dx + 4, 4) * 4 + lax.rem(y + dy + 4, 4)

    sib = dev(z, 1 - c, h)
    after = {"seq": lax.rem(s + 1, 32), "hid": h}
    extra = {"seq": lax.rem(s + 2 * c - 1 + 32, 32), "hid": h}

    load_act = pltpu.make_async_copy(act_hbm, act.at[pl.ds(HALO, TOK), :], local_sem.at[0])
    own_rows = pl.ds(pl.multiple_of(s * 128, 128), 128)
    load_in = pltpu.make_async_copy(wi_hbm, w_in.at[own_rows, :], local_sem.at[1])
    load_gate = pltpu.make_async_copy(wg_hbm, w_gate.at[own_rows, :], local_sem.at[2])
    group_cols = pl.ds(pl.multiple_of(x * 256 + (y // 2) * 128, 128), 128)
    small = [
        pltpu.make_async_copy(src, dst, small_sem.at[i])
        for i, (src, dst) in enumerate(
            (
                (wgr_hbm.at[:, group_cols], wgr_ref),
                (wst_hbm, wst_ref),
                (wo_hbm, wo_ref),
                (gain_hbm, gain_ref),
                (tapi_hbm, tapi_ref),
                (tapg_hbm.at[:, group_cols], tapg_ref),
                (bias_hbm, bias_ref),
                (decay_hbm, decay_ref),
                (skip_hbm, skip_ref),
            )
        )
    ]
    load_in.start()
    for item in small:
        item.start()
    load_gate.start()
    load_act.start()

    barrier = pltpu.get_barrier_semaphore()
    for step in (1, -1, 2, -2):
        pl.semaphore_signal(barrier, inc=1, device_id=dev(zmod(z + step), c, h), device_id_type=MESH)
    pl.semaphore_signal(barrier, inc=1, device_id=sib, device_id_type=MESH)
    pl.semaphore_signal(barrier, inc=1, device_id=extra, device_id_type=MESH)
    for step in (1, 2, 3):
        for hh in (hid_at(step, 0), hid_at(0, step)):
            pl.semaphore_signal(barrier, inc=1, device_id=dev(z, c, hh), device_id_type=MESH)

    for item in small:
        item.wait()
    tile = wgr_ref[...].astype(F32).T
    half = jnp.where(y % 2 == 0, tile[:64], tile[64:])
    steps_t = wst_ref[...].astype(F32)
    mine = jnp.where(
        x < 2,
        jnp.where(x == 0, steps_t[0:16], steps_t[16:32]),
        jnp.where(x == 2, steps_t[32:48], steps_t[48:64]),
    )
    own_lanes = pl.ds(pl.multiple_of(s * 128, 128), 128)
    w_gs[0:64, own_lanes] = half.astype(BF16)
    w_gs[64:80, own_lanes] = mine.astype(BF16)

    pl.semaphore_wait(barrier, 12)

    send_halo = remote(
        act_hbm.at[pl.ds(TOK - HALO, HALO), :],
        act.at[pl.ds(0, HALO), :],
        halo_sem.at[0],
        halo_sem.at[1],
        after,
    )

    def block(p, zz):
        row = pl.multiple_of((2 * zz + c) * 128, 128)
        if p == 0:
            return w_gs.at[:, pl.ds(row, 128)]
        part = 64 * ((p - 1) % 2)
        if p < 3:
            return w_in.at[pl.ds(row + part, 64), :]
        return w_gate.at[pl.ds(row + part, 64), :]

    def sib_block(p, zz):
        row = pl.multiple_of((2 * zz + 1 - c) * 128, 128)
        if p == 0:
            return w_gs.at[:, pl.ds(row, 128)]
        part = 64 * ((p - 1) % 2)
        if p < 3:
            return w_in.at[pl.ds(row + part, 64), :]
        return w_gate.at[pl.ds(row + part, 64), :]

    def origin(d, k):
        return zmod(z - k) if d == 0 else zmod(z + k)

    def ring(p, d, k, recv_k):
        ref = block(p, origin(d, k))
        target = zmod(z + 1) if d == 0 else zmod(z - 1)
        return remote(ref, ref, zs.at[p, d, k], zr.at[p, d, recv_k], dev(target, c, h))

    def to_sib(p, d, k):
        ref = block(p, origin(d, k))
        return remote(ref, ref, bs.at[p, d, k], br.at[p, d, k], sib)

    def from_sib(p, d, k):
        ref = sib_block(p, origin(d, k))
        remote(ref, ref, bs.at[p, d, k], br.at[p, d, k], sib).wait_recv()

    keeper = z % 4
    is_source = keeper == y

    def out_rows(zz, cc):
        return pl.multiple_of((zz // 4) * 256 + 128 * cc, 128)

    def out_part(a, zz, cc, column):
        return w_out.at[
            pl.ds(out_rows(zz, cc) + 64 * a, 64), pl.ds(pl.multiple_of(256 * column, 256), 256)
        ]

    def bring(column):
        return remote(
            land,
            w_out.at[pl.ds(out_rows(z, c), 128), pl.ds(pl.multiple_of(256 * column, 256), 256)],
            cs.at[0],
            cr.at[column],
            dev(z, c, x * 4 + keeper),
        )

    near = tuple((d + 3) % 4 + 1 for d in (z - y + 16, y - z + 16))
    OUT_FAR = ((8, 7), (7, 8))

    def out_dist(d, q):
        return near[d] + 4 * (q // 4)

    def out_origin(d, q):
        return zmod(z - out_dist(d, q)) if d == 0 else zmod(z + out_dist(d, q))

    def out_send(a, d, zz, column, slot):
        ref = out_part(a, zz, c, column)
        target = zmod(z + 1) if d == 0 else zmod(z - 1)
        return remote(ref, ref, os_.at[a, d, slot], orr.at[a, d, slot], dev(target, c, h))

    def out_to_sib(a, d, zz, column, slot):
        ref = out_part(a, zz, c, column)
        return remote(ref, ref, ws.at[a, d, slot], wr.at[a, d, slot], sib)

    def next_slot(d, q):
        return jnp.where(near[d] < 4, q, q + 4)

    def serve_out(t):
        if t == 0:

            @pl.when(is_source)
            def _():
                for step in (1, 2, 3):
                    bring(lax.rem(y + step, 4)).wait_recv()

        if t < 4:

            @pl.when(is_source)
            def _():
                for a in (0, 1):
                    for d in (0, 1):
                        out_send(a, d, z, t, t).start()
                    out_to_sib(a, 2, z, t, t).start()

        if t > 0:
            for a in (0, 1):
                for d in (0, 1):
                    q = t - near[d]
                    reach = out_dist(d, q)

                    @pl.when((q >= 0) & (q < 8) & (reach <= OUT_FAR[a][d]))
                    def _():
                        zz, column = out_origin(d, q), q % 4
                        out_send(a, d, zz, column, q).wait_recv()

                        @pl.when(reach < OUT_FAR[a][d])
                        def _():
                            out_send(a, d, zz, column, next_slot(d, q)).start()

                        out_to_sib(a, d, zz, column, q).start()

    def out_end(q, carry):
        for a in (0, 1):
            for d in (0, 1):
                reach = out_dist(d, q)

                @pl.when(reach <= OUT_FAR[a][d])
                def _():
                    zz, column = out_origin(d, q), q % 4
                    theirs = out_part(a, zz, 1 - c, column)
                    remote(theirs, theirs, ws.at[a, d, q], wr.at[a, d, q], sib).wait_recv()

        return carry

    def out_own_end():
        @pl.when(is_source)
        def _():
            for a in (0, 1):
                for column in range(4):
                    theirs = out_part(a, z, 1 - c, column)
                    remote(theirs, theirs, ws.at[a, 2, column], wr.at[a, 2, column], sib).wait_recv()

    def out_drain(q, carry):
        for a in (0, 1):
            for d in (0, 1):
                reach = out_dist(d, q)

                @pl.when(reach <= OUT_FAR[a][d])
                def _():
                    zz, column = out_origin(d, q), q % 4

                    @pl.when(reach < OUT_FAR[a][d])
                    def _():
                        out_send(a, d, zz, column, next_slot(d, q)).wait_send()

                    out_to_sib(a, d, zz, column, q).wait_send()

        return carry

    def out_own_drain():
        @pl.when(is_source)
        def _():
            for a in (0, 1):
                for column in range(4):
                    for d in (0, 1):
                        out_send(a, d, z, column, column).wait_send()
                    out_to_sib(a, 2, z, column, column).wait_send()

        @pl.when(jnp.logical_not(is_source))
        def _():
            bring(y).wait_send()

    def hand_on(p, d, k):
        to_sib(p, d, k).start()

    def first(p):
        ring(p, 0, 0, 1).start()
        ring(p, 1, 0, 1).start()
        hand_on(p, 0, 0)

    def event(p, d, k, forward):
        ring(p, d, k, k).wait_recv()
        if forward:
            ring(p, d, k, k + 1).start()
        hand_on(p, d, k)

    def columns(zz):
        return pl.ds(pl.multiple_of(zz * 256, 256), 256)

    def dots_in(*planes):
        acc_i[...] += sum(
            jnp.dot(act[:, columns(zz)], w_in[columns(zz), :], preferred_element_type=F32)
            for zz in planes
        )

    def dots_gs(*planes):
        acc_s[...] += sum(
            lax.dot_general(
                act[:, columns(zz)],
                w_gs[:, columns(zz)],
                (((1,), (1,)), ((), ())),
                preferred_element_type=F32,
            )
            for zz in planes
        )

    def gate_dots(*planes):
        acc_g[...] += sum(
            jnp.dot(act[HALO:, columns(zz)], w_gate[columns(zz), :], preferred_element_type=F32)
            for zz in planes
        )

    first(0)
    load_in.wait()
    first(1)
    first(2)
    send_halo.start()
    load_gate.wait()
    first(3)
    scaled = (wo_ref[...].astype(F32) * gain_ref[...]).astype(BF16)

    @pl.when(is_source)
    def _():
        w_out[pl.ds(out_rows(z, c), 128), pl.ds(pl.multiple_of(256 * y, 256), 256)] = scaled

    @pl.when(jnp.logical_not(is_source))
    def _():
        land[...] = scaled
        bring(y).start()

    acc_i[...] = jnp.zeros_like(acc_i)
    acc_s[...] = jnp.zeros_like(acc_s)
    acc_g[...] = jnp.zeros_like(acc_g)

    def serve(pieces, k):
        for p in pieces:
            for d in (0, 1):
                if k <= FAR[p][d]:
                    event(p, d, k, k < FAR[p][d])

    def use(pieces, dots, k):
        for p in pieces:
            for d in (0, 1):
                if k <= FAR[p][d]:
                    from_sib(p, d, k)
        if k < 8:
            dots(origin(0, k), origin(1, k))
        else:
            dots(origin(0, k))

    IN = (1, 2)
    GATE = (3, 4)

    serve((0,), 1)
    serve(IN, 1)
    load_act.wait()
    send_halo.wait()
    for p in (0, 1, 2):
        from_sib(p, 0, 0)
    dots_gs(z)
    dots_in(z)
    for k in (2, 3, 4, 5, 6, 7):
        serve((0, 1), k)
        use((0,), dots_gs, k - 1)
        serve((2,), k)
        use(IN, dots_in, k - 1)
        serve((3,), k - 1)
    serve((0,), 8)
    first(4)
    serve_out(0)
    use((0,), dots_gs, 7)
    use((0,), dots_gs, 8)

    not_first = jnp.where(s == 0, 0.0, 1.0).astype(F32)
    lane128 = lax.broadcasted_iota(jnp.int32, (TOK, 128), 1)
    raw = acc_s[HALO:, :]
    acc_s[...] = acc_s[...].astype(BF16).astype(F32)
    acc_s[0:HALO, :] = acc_s[0:HALO, :] * not_first
    tap_tile = tapg_ref[...]
    tap_g = jnp.where(y % 2 == 0, tap_tile, pltpu.roll(tap_tile, 64, axis=1))
    conv = jnp.zeros((TOK, 80), F32)
    for position in range(4):
        conv = conv + acc_s[pl.ds(HALO - 3 + position, TOK), :] * tap_g[position : position + 1, :80]
    conv = conv * jax.nn.sigmoid(conv)
    both = jnp.where(lane128[:, :80] < 64, conv, raw)
    both_t = jnp.concatenate([both, jnp.zeros((TOK, 48), F32)], axis=1).T
    own_cols = pl.ds(pl.multiple_of(64 * y, 64), 64)
    bct[own_cols, :] = both_t[0:64].astype(BF16)

    def y_copy(j, where):
        rows = bct.at[pl.ds(pl.multiple_of(64 * where, 64), 64), :]
        return remote(rows, rows, ys.at[j - 1], yr.at[j - 1], dev(z, c, hid_at(0, j)))

    for j in (1, 3, 2):
        y_copy(j, y).start()

    serve(IN, 8)
    serve((3,), 7)
    use(IN, dots_in, 7)

    step4 = jnp.where(
        y < 2,
        jnp.where(y == 0, both_t[64:68], both_t[68:72]),
        jnp.where(y == 2, both_t[72:76], both_t[76:80]),
    )
    step8 = jnp.concatenate([step4, step4], axis=0)
    head = lax.broadcasted_iota(jnp.int32, (8, TOK), 0) % 4
    lane = lax.broadcasted_iota(jnp.int32, (8, TOK), 1)

    def per_head(ref):
        return jnp.where(
            head < 2, jnp.where(head == 0, ref[0], ref[1]), jnp.where(head == 2, ref[2], ref[3])
        )

    v = step8 + per_head(bias_ref)
    dt = jnp.maximum(v, 0.0) + jnp.log1p(jnp.exp(-jnp.abs(v)))
    cum = dt * -jnp.exp(per_head(decay_ref))
    for shift in (1, 2, 4, 8, 16, 32, 64, 128):
        cum = cum + jnp.where(lane % 256 >= shift, pltpu.roll(cum, shift, axis=1), 0.0)
    last = jnp.where(lane < 256, cum[:, 255:256], cum[:, 511:512])
    weight = jnp.exp(last - cum) * dt
    stack = jnp.concatenate([cum, weight, jnp.exp(cum), jnp.zeros((104, TOK), F32)], axis=0)
    cols[...] = stack.T

    def expand(q):
        halves = []
        for i in (0, 2):
            lo = jnp.broadcast_to(cols[:, 8 * q + i : 8 * q + i + 1], (TOK, 128))
            hi = jnp.broadcast_to(cols[:, 8 * q + i + 1 : 8 * q + i + 2], (TOK, 128))
            halves.append(jnp.where(lane128 < 64, lo, hi))
        return jnp.concatenate(halves, axis=1)

    use(IN, dots_in, 8)
    serve((3,), 8)
    serve((4,), 1)
    serve_out(1)
    acc_i[...] = acc_i[...].astype(BF16).astype(F32)
    acc_i[0:HALO, :] = acc_i[0:HALO, :] * not_first
    conv = jnp.zeros((TOK, 256), F32)
    for position in range(4):
        conv = conv + acc_i[pl.ds(HALO - 3 + position, TOK), :] * tapi_ref[position : position + 1, :]
    conv = conv * jax.nn.sigmoid(conv)
    xc[...] = conv.astype(BF16)

    head_lane = lax.broadcasted_iota(jnp.int32, (1, 256), 1) // 64
    weighted = (xc[...].astype(F32) * expand(1)).astype(BF16)
    expcum = expand(2)
    decay0 = expcum[255:256]
    decay1 = expcum[511:512]

    for j in (1, 2, 3):
        y_copy(j, lax.rem(y + 4 - j, 4)).wait()

    fresh0 = jnp.dot(bct[0:128, 0:256], weighted[0:256], preferred_element_type=F32)
    fresh1 = jnp.dot(bct[0:128, 256:512], weighted[256:512], preferred_element_type=F32)
    end_own = decay1 * fresh0 + fresh1
    total_own = decay0 * decay1
    th, tl = split(jnp.broadcast_to(total_own, (8, 256)))
    tail = jnp.concatenate([th.astype(F32), tl.astype(F32)], axis=0).astype(BF16)
    e_own[0:128, :] = end_own.astype(BF16)
    e_own[128:144, :] = tail
    swap = remote(e_own, e_sib, es.at[0], es.at[1], sib)
    swap.start()

    serve((4,), 2)
    serve_out(2)
    swap.wait()

    end_sib = e_sib[0:128, :].astype(F32)
    total_sib = e_sib[128:129, :].astype(F32) + e_sib[136:137, :].astype(F32)

    def my_half(value):
        return jnp.where(c == 0, value[:, 0:128], value[:, 128:256])

    second_decay = jnp.where(c == 0, total_sib, total_own)
    chip_end = second_decay * jnp.where(c == 0, end_own, end_sib) + jnp.where(
        c == 0, end_sib, end_own
    )
    chip_total = jnp.broadcast_to(my_half(total_own * total_sib), (8, 128))
    th, tl = split(chip_total)
    tbuf[z, 0:128, :] = my_half(chip_end).astype(BF16)
    tbuf[z, 128:144, :] = jnp.concatenate([th.astype(F32), tl.astype(F32)], axis=0).astype(BF16)

    def t_send(d, k, hop):
        ref = tbuf.at[origin(d, k)]
        target = zmod(z + hop) if d == 0 else zmod(z - hop)
        return remote(ref, ref, ts.at[hop - 1, d, k], tr.at[d, k + hop], dev(target, c, h))

    def t_recv(d, k):
        ref = tbuf.at[origin(d, k)]
        remote(ref, ref, ts.at[0, d, k], tr.at[d, k], sib).wait_recv()

    sent = []

    def t_start(d, k, hop):
        t_send(d, k, hop).start()
        sent.append((d, k, hop))

    for hop in (2, 1):
        for d in (0, 1):
            t_start(d, 0, hop)

    row = lax.broadcasted_iota(jnp.int32, (256, 256), 0)
    column = lax.broadcasted_iota(jnp.int32, (256, 256), 1)
    c_mat = bct[128:256, :].astype(F32).T.astype(BF16)
    intra = []

    def span(q):
        tokens = slice(256 * q, 256 * q + 256)
        scores = jnp.dot(c_mat[tokens], bct[0:128, tokens], preferred_element_type=F32)
        scores = jnp.where(row >= column, scores, 0.0)
        total = jnp.zeros((256, 256), F32)
        for i in range(4):
            gap = jnp.minimum(cols[tokens, i : i + 1] - cum[i : i + 1, tokens], 0.0)
            mixing = (scores * jnp.exp(gap) * dt[i : i + 1, tokens]).astype(BF16)
            x_head = jnp.where(head_lane == i, xc[tokens, :].astype(F32), 0.0).astype(BF16)
            total = total + jnp.dot(mixing, x_head, preferred_element_type=F32)
        return total

    mixed0 = span(0)
    serve((4,), 3)
    serve_out(3)
    for d in (0, 1):
        t_recv(d, 2)
        for hop in (2, 1):
            t_start(d, 2, hop)
    serve((4,), 4)
    mixed1 = span(1)
    serve_out(4)
    skip = jnp.where(
        head_lane < 2,
        jnp.where(head_lane == 0, skip_ref[0], skip_ref[1]),
        jnp.where(head_lane == 2, skip_ref[2], skip_ref[3]),
    )
    xf = xc[...].astype(F32)
    mixed0 = mixed0 + skip * xf[0:256]
    mixed1 = mixed1 + skip * xf[256:512]
    for d in (0, 1):
        t_recv(d, 4)
        for hop in (2, 1):
            t_start(d, 4, hop)
    serve((4,), 5)
    serve_out(5)
    for p in GATE:
        from_sib(p, 0, 0)
    gate_dots(z)
    for k in (1, 2, 3, 4):
        use(GATE, gate_dots, k)
    t_recv(0, 6)
    for hop in (2, 1):
        t_start(0, 6, hop)
    t_recv(1, 6)
    t_start(1, 6, 1)
    serve((4,), 6)
    serve_out(6)
    use(GATE, gate_dots, 5)
    serve((4,), 7)
    serve_out(7)
    use(GATE, gate_dots, 6)
    for d, ks in ((0, (1, 3, 5, 7, 8)), (1, (1, 3, 5, 7))):
        for k in ks:
            t_recv(d, k)

    prefix = jnp.zeros((128, 128), F32)
    for k in range(15, 0, -1):
        zz = zmod(z - k)
        decay = tbuf[zz, 128:129, :].astype(F32) + tbuf[zz, 136:137, :].astype(F32)
        joined = decay * prefix + tbuf[zz, 0:128, :].astype(F32)
        prefix = jnp.where(z >= k, joined, prefix)
    pbuf[...] = prefix
    swap2 = remote(pbuf, psib, es.at[2], es.at[3], sib)
    swap2.start()
    serve((4,), 8)
    use(GATE, gate_dots, 7)
    use(GATE, gate_dots, 8)
    swap2.wait()
    other = psib[...]
    before = jnp.where(
        c == 0,
        jnp.concatenate([prefix, other], axis=1),
        jnp.concatenate([other, prefix], axis=1),
    )
    state0 = jnp.where(c == 0, before, total_sib * before + end_sib)
    state1 = decay0 * state0 + fresh0

    def gated(q, mixed, state):
        tokens = slice(256 * q, 256 * q + 256)
        high, low = split(state)
        inter = jnp.dot(c_mat[tokens], high, preferred_element_type=F32)
        inter = inter + jnp.dot(c_mat[tokens], low, preferred_element_type=F32)
        mixed = mixed + inter * expcum[tokens]
        gate = acc_g[tokens, :].astype(BF16).astype(F32)
        gath[tokens, pl.ds(pl.multiple_of(256 * y, 256), 256)] = (
            mixed * (gate * jax.nn.sigmoid(gate))
        ).astype(BF16)

    def part(u, a, first_row, rows):
        column = pl.multiple_of(256 * lax.rem(y + a + 4, 4), 256)
        return gath.at[pl.ds(128 * u + first_row, rows), pl.ds(column, 256)]

    STEP = (1, -1)

    def g_near(u, way, a):
        ref = part(u, a, 0, 128)
        return remote(ref, ref, gs.at[u, way], gr.at[u, way], dev(z, c, hid_at(0, STEP[way])))

    def g_far(u, way, a):
        ref = part(u, a, 64 * way, 64)
        return remote(
            ref, ref, gs.at[u, 2 + way], gr.at[u, 2 + way], dev(z, c, hid_at(0, STEP[way]))
        )

    def near_start(u):
        for way in (0, 1):
            g_near(u, way, 0).start()

    def near_take(u):
        for way in (0, 1):
            g_near(u, way, -STEP[way]).wait_recv()
            g_far(u, way, -STEP[way]).start()

    gated(0, mixed0, state0)
    near_start(0)
    near_start(1)
    gated(1, mixed1, state1)
    near_start(2)
    serve_out(8)

    def drain_weights():
        for p in range(5):
            for d in (0, 1):

                def drain(k, carry):
                    ring(p, d, k, k + 1).wait_send()
                    return carry

                lax.fori_loop(0, FAR[p][d], drain, 0)

                def drain_sib(k, carry):
                    to_sib(p, d, k).wait_send()
                    return carry

                lax.fori_loop(d, FAR[p][d] + 1, drain_sib, 0)

    near_take(0)
    near_take(1)
    near_start(3)
    serve_out(9)
    near_take(2)
    serve_out(10)
    near_take(3)
    serve_out(11)
    lax.fori_loop(0, 8, out_end, 0)
    out_own_end()

    def product(u, offset):
        rows = pl.ds(pl.multiple_of(256 * lax.rem(x + offset, 4), 256), 256)
        return lax.dot_general(
            gath[256 * u : 256 * u + 256, :],
            w_out[rows, :],
            (((1,), (1,)), ((), ())),
            preferred_element_type=F32,
        )

    def along(u, slot, way, src, dst):
        return remote(
            src, dst, hs.at[u, slot, way], hr.at[u, slot, way], dev(z, c, hid_at(STEP[way], 0))
        )

    top = pl.ds(0, 128)
    low = pl.ds(128, 128)

    def far_send(u, way):
        return along(u, 0, way, s_far.at[u, (top, low)[way]], (r_up, r_down)[way].at[u])

    def early_send(u, way):
        rows = (low, top)[way]
        return along(u, 1, way, (s_up, s_down)[way].at[u, rows], (f_up, f_down)[way].at[u, rows])

    def late_send(u, way):
        rows = (top, low)[way]
        return along(u, 2, way, (s_up, s_down)[way].at[u, rows], (f_up, f_down)[way].at[u, rows])

    def square_send(u, j):
        return remote(
            sq_own.at[u], sq_in.at[u, j - 1], qs.at[u, j - 1], qr.at[u, j - 1], dev(z, c, hid_at(j, 0))
        )

    def multiply_far(u):
        s_far[u] = product(u, 2).astype(BF16)
        for way in (0, 1):
            far_send(u, way).start()

    def multiply_near(u):
        up = product(u, 1)
        s_up[u, 128:256, :] = up[128:256].astype(BF16)
        early_send(u, 0).start()
        p_up[u] = up[0:128]
        down = product(u, 3)
        s_down[u, 0:128, :] = down[0:128].astype(BF16)
        early_send(u, 1).start()
        p_down[u] = down[128:256]

    def square(u):
        total = jnp.zeros((256, 128), F32)
        for i in range(8):
            g = gath[256 * u : 256 * u + 256, 128 * i : 128 * i + 128].astype(F32)
            total = total + g * g
        sq_own[u] = jnp.broadcast_to(jnp.sum(total.T, axis=0, keepdims=True), (8, 256))
        for j in (1, 3, 2):
            square_send(u, j).start()

    def add(u):
        far_send(u, 0).wait_recv()
        s_up[u, 0:128, :] = (p_up[u] + r_up[u].astype(F32)).astype(BF16)
        late_send(u, 0).start()
        far_send(u, 1).wait_recv()
        s_down[u, 128:256, :] = (p_down[u] + r_down[u].astype(F32)).astype(BF16)
        late_send(u, 1).start()

    def finish(u):
        for j in (1, 2, 3):
            square_send(u, j).wait_recv()
        squares = sq_own[u] + sq_in[u, 0] + sq_in[u, 1] + sq_in[u, 2]
        scale = lax.rsqrt(squares / INNER + 1e-5)
        scale = jnp.broadcast_to(scale[0:1], (128, 256)).T
        for way in (0, 1):
            early_send(u, way).wait_recv()
            late_send(u, way).wait_recv()
        value = p_own[u] + f_up[u].astype(F32) + f_down[u].astype(F32)
        for half_of in (0, 128):
            out_ref[256 * u : 256 * u + 256, half_of : half_of + 128] = (
                value[:, half_of : half_of + 128] * scale
            ).astype(BF16)

    for u in range(4):
        for way in (0, 1):
            g_far(u, way, 2).wait_recv()
        if u % 2 == 1:
            multiply_far(u // 2)
            multiply_near(u // 2)
    square(0)
    add(0)
    p_own[0] = product(0, 0)
    square(1)
    add(1)
    p_own[1] = product(1, 0)
    drain_weights()
    lax.fori_loop(0, 8, out_drain, 0)
    out_own_drain()
    for d, k, hop in sent:
        t_send(d, k, hop).wait_send()
    finish(0)
    finish(1)
    for u in range(4):
        for way in (0, 1):
            g_near(u, way, 0).wait_send()
            g_far(u, way, -STEP[way]).wait_send()
    for u in (0, 1):
        for way in (0, 1):
            far_send(u, way).wait_send()
            early_send(u, way).wait_send()
            late_send(u, way).wait_send()
        for j in (1, 2, 3):
            square_send(u, j).wait_send()


def local(
    activations,
    w_inner,
    w_gate,
    w_groups,
    w_step,
    w_out,
    conv_inner,
    conv_groups,
    step_bias,
    decay_log,
    skip_gain,
    norm_gain,
):
    anywhere = pl.BlockSpec(memory_space=pl.ANY)
    vmem = pl.BlockSpec(memory_space=pltpu.VMEM)
    dma = pltpu.SemaphoreType.DMA
    return pl.pallas_call(
        kernel,
        out_shape=jax.ShapeDtypeStruct((TOK, 256), BF16),
        in_specs=[anywhere] * 12,
        out_specs=vmem,
        scratch_shapes=[
            pltpu.VMEM((128, 256), BF16),
            pltpu.VMEM((128, 128), BF16),
            pltpu.VMEM((64, 128), BF16),
            pltpu.VMEM((4, 256), F32),
            pltpu.VMEM((4, 128), F32),
            pltpu.SMEM((4,), F32),
            pltpu.SMEM((4,), F32),
            pltpu.SMEM((4,), F32),
            pltpu.VMEM((1, 256), F32),
            dma((9,)),
            pltpu.VMEM((HALO + TOK, 4096), BF16),
            pltpu.VMEM((4096, 256), BF16),
            pltpu.VMEM((4096, 256), BF16),
            pltpu.VMEM((80, 4096), BF16),
            pltpu.VMEM((128, 256), BF16),
            pltpu.VMEM((1024, 1024), BF16),
            pltpu.VMEM((TOK, 1024), BF16),
            pltpu.VMEM((2, 8, 256), F32),
            pltpu.VMEM((2, 3, 8, 256), F32),
            pltpu.VMEM((2, 128, 256), F32),
            pltpu.VMEM((2, 128, 256), F32),
            pltpu.VMEM((2, 256, 256), F32),
            pltpu.VMEM((2, 256, 256), BF16),
            pltpu.VMEM((2, 256, 256), BF16),
            pltpu.VMEM((2, 256, 256), BF16),
            pltpu.VMEM((2, 128, 256), BF16),
            pltpu.VMEM((2, 128, 256), BF16),
            pltpu.VMEM((2, 256, 256), BF16),
            pltpu.VMEM((2, 256, 256), BF16),
            pltpu.VMEM((HALO + TOK, 256), F32),
            pltpu.VMEM((TOK, 256), F32),
            pltpu.VMEM((HALO + TOK, 80), F32),
            pltpu.VMEM((256, TOK), BF16),
            pltpu.VMEM((TOK, 256), BF16),
            pltpu.VMEM((TOK, 128), F32),
            pltpu.VMEM((144, 256), BF16),
            pltpu.VMEM((144, 256), BF16),
            pltpu.VMEM((16, 144, 128), BF16),
            pltpu.VMEM((128, 128), F32),
            pltpu.VMEM((128, 128), F32),
            dma((3,)),
            dma((2,)),
            dma((5, 2, 9)),
            dma((5, 2, 9)),
            dma((5, 2, 9)),
            dma((5, 2, 9)),
            dma((1,)),
            dma((4,)),
            dma((2, 2, 8)),
            dma((2, 2, 8)),
            dma((2, 3, 8)),
            dma((2, 3, 8)),
            dma((3,)),
            dma((3,)),
            dma((4,)),
            dma((2, 2, 9)),
            dma((2, 9)),
            dma((4, 4)),
            dma((4, 4)),
            dma((2, 3)),
            dma((2, 3)),
            dma((2, 3, 2)),
            dma((2, 3, 2)),
        ],
        compiler_params=pltpu.CompilerParams(
            collective_id=0, has_side_effects=True, vmem_limit_bytes=67043328
        ),
    )(
        activations,
        w_inner,
        w_gate,
        w_out,
        w_groups,
        w_step.T,
        conv_inner,
        conv_groups,
        step_bias,
        decay_log,
        skip_gain,
        norm_gain.reshape(1, 256),
    )


def solution(mesh):
    in_specs = (
        P("seq", None),
        P("seq", "hid"),
        P("seq", "hid"),
        P("seq", None),
        P("seq", None),
        P("seq", "hid"),
        P(None, "hid"),
        P(),
        P("hid"),
        P("hid"),
        P("hid"),
        P("hid"),
    )
    return jax.shard_map(
        local, mesh=mesh, in_specs=in_specs, out_specs=P("seq", "hid"), check_vma=False
    )
```

```python
import jax
import jax.numpy as jnp
from jax import lax
from jax.experimental import pallas as pl
from jax.experimental.pallas import tpu as pltpu
from jax.sharding import PartitionSpec as P

F32 = jnp.float32
BF16 = jnp.bfloat16
MESH = pl.DeviceIdType.MESH
INNER = 4096
TOK = 512
HALO = 8
NZ = 16
FAR = ((8, 7), (8, 7), (7, 8), (8, 7), (7, 8))
KIND = (0, 1, 1, 2, 2)


def remote(src, dst, send, recv, device):
    return pltpu.make_async_remote_copy(
        src_ref=src, dst_ref=dst, send_sem=send, recv_sem=recv, device_id=device, device_id_type=MESH
    )


def split(value):
    high = value.astype(BF16)
    return high, (value - high.astype(F32)).astype(BF16)


def kernel(
    act_hbm,
    wi_hbm,
    wg_hbm,
    wo_hbm,
    wgr_hbm,
    wst_hbm,
    tapi_hbm,
    tapg_hbm,
    bias_hbm,
    decay_hbm,
    skip_hbm,
    gain_hbm,
    out_ref,
    wo_ref,
    wgr_ref,
    wst_ref,
    tapi_ref,
    tapg_ref,
    bias_ref,
    decay_ref,
    skip_ref,
    gain_ref,
    small_sem,
    act,
    w_in,
    w_gate,
    w_gs,
    land,
    w_out,
    gath,
    sq_own,
    sq_in,
    p_up,
    p_down,
    p_own,
    s_far,
    s_up,
    s_down,
    r_up,
    r_down,
    f_up,
    f_down,
    acc_i,
    acc_g,
    acc_s,
    bct,
    xc,
    cols,
    e_own,
    e_sib,
    tbuf,
    pbuf,
    psib,
    local_sem,
    halo_sem,
    zs,
    zr,
    bs,
    br,
    br_gate,
    cs,
    cr,
    os_,
    orr,
    ws,
    wr,
    ys,
    yr,
    es,
    ts,
    tr,
    gs,
    gr,
    qs,
    qr,
    hs,
    hr,
):
    s = lax.axis_index("seq")
    h = lax.axis_index("hid")
    z = s // 2
    c = s % 2
    x = h // 4
    y = h % 4

    def dev(zz, cc, hh):
        return {"seq": 2 * zz + cc, "hid": hh}

    def zmod(v):
        return lax.rem(v + 2 * NZ, NZ)

    def hid_at(dx, dy):
        return lax.rem(x + dx + 4, 4) * 4 + lax.rem(y + dy + 4, 4)

    sib = dev(z, 1 - c, h)
    after = {"seq": lax.rem(s + 1, 32), "hid": h}
    extra = {"seq": lax.rem(s + 2 * c - 1 + 32, 32), "hid": h}

    load_act = pltpu.make_async_copy(act_hbm, act.at[pl.ds(HALO, TOK), :], local_sem.at[0])
    own_rows = pl.ds(pl.multiple_of(s * 128, 128), 128)
    load_in = pltpu.make_async_copy(wi_hbm, w_in.at[own_rows, :], local_sem.at[1])
    load_gate = pltpu.make_async_copy(wg_hbm, w_gate.at[own_rows, :], local_sem.at[2])
    group_cols = pl.ds(pl.multiple_of(x * 256 + (y // 2) * 128, 128), 128)
    small = [
        pltpu.make_async_copy(src, dst, small_sem.at[i])
        for i, (src, dst) in enumerate(
            (
                (wgr_hbm.at[:, group_cols], wgr_ref),
                (wst_hbm, wst_ref),
                (wo_hbm, wo_ref),
                (gain_hbm, gain_ref),
                (tapi_hbm, tapi_ref),
                (tapg_hbm.at[:, group_cols], tapg_ref),
                (bias_hbm, bias_ref),
                (decay_hbm, decay_ref),
                (skip_hbm, skip_ref),
            )
        )
    ]
    load_in.start()
    for item in small:
        item.start()
    load_gate.start()
    load_act.start()

    barrier = pltpu.get_barrier_semaphore()
    for step in (1, -1, 2, -2):
        pl.semaphore_signal(barrier, inc=1, device_id=dev(zmod(z + step), c, h), device_id_type=MESH)
    pl.semaphore_signal(barrier, inc=1, device_id=sib, device_id_type=MESH)
    pl.semaphore_signal(barrier, inc=1, device_id=extra, device_id_type=MESH)
    for step in (1, 2, 3):
        for hh in (hid_at(step, 0), hid_at(0, step)):
            pl.semaphore_signal(barrier, inc=1, device_id=dev(z, c, hh), device_id_type=MESH)

    for item in small:
        item.wait()
    tile = wgr_ref[...].astype(F32).T
    half = jnp.where(y % 2 == 0, tile[:64], tile[64:])
    steps_t = wst_ref[...].astype(F32)
    mine = jnp.where(
        x < 2,
        jnp.where(x == 0, steps_t[0:16], steps_t[16:32]),
        jnp.where(x == 2, steps_t[32:48], steps_t[48:64]),
    )
    own_lanes = pl.ds(pl.multiple_of(s * 128, 128), 128)
    w_gs[0:64, own_lanes] = half.astype(BF16)
    w_gs[64:80, own_lanes] = mine.astype(BF16)

    pl.semaphore_wait(barrier, 12)

    send_halo = remote(
        act_hbm.at[pl.ds(TOK - HALO, HALO), :],
        act.at[pl.ds(0, HALO), :],
        halo_sem.at[0],
        halo_sem.at[1],
        after,
    )

    def sent_all(sem, ref):
        remote(ref, ref, sem, sem, sib).wait_send()

    def got_all(sem, ref):
        remote(ref, ref, sem, sem, sib).wait_recv()

    def block(p, zz):
        row = pl.multiple_of((2 * zz + c) * 128, 128)
        if p == 0:
            return w_gs.at[:, pl.ds(row, 128)]
        part = 64 * ((p - 1) % 2)
        if p < 3:
            return w_in.at[pl.ds(row + part, 64), :]
        return w_gate.at[pl.ds(row + part, 64), :]

    def sib_block(kind, zz):
        row = pl.multiple_of((2 * zz + 1 - c) * 128, 128)
        if kind == 0:
            return w_gs.at[:, pl.ds(row, 128)]
        return w_in.at[pl.ds(row, 128), :]

    def origin(d, k):
        return zmod(z - k) if d == 0 else zmod(z + k)

    def ring(p, d, k, recv_k):
        ref = block(p, origin(d, k))
        target = zmod(z + 1) if d == 0 else zmod(z - 1)
        return remote(ref, ref, zs.at[KIND[p]], zr.at[p, d, recv_k - 1], dev(target, c, h))

    def to_sib(p, d, k):
        ref = block(p, origin(d, k))
        kind = KIND[p]
        landed = br_gate.at[0] if kind == 2 else br.at[kind, 0 if k == 8 else d, k]
        return remote(ref, ref, bs.at[kind], landed, sib)

    def from_sib(kind, d, k):
        got_all(br.at[kind, d, k], sib_block(kind, origin(d, k)))

    keeper = z % 4
    is_source = keeper == y

    def out_rows(zz, cc):
        return pl.multiple_of((zz // 4) * 256 + 128 * cc, 128)

    def out_part(a, zz, cc, column):
        return w_out.at[
            pl.ds(out_rows(zz, cc) + 64 * a, 64), pl.ds(pl.multiple_of(256 * column, 256), 256)
        ]

    def bring(column):
        return remote(
            land,
            w_out.at[pl.ds(out_rows(z, c), 128), pl.ds(pl.multiple_of(256 * column, 256), 256)],
            cs.at[0],
            cr.at[0],
            dev(z, c, x * 4 + keeper),
        )

    near = tuple((d + 3) % 4 + 1 for d in (z - y + 16, y - z + 16))
    OUT_FAR = ((8, 7), (7, 8))

    def out_dist(d, q):
        return near[d] + 4 * (q // 4)

    def out_origin(d, q):
        return zmod(z - out_dist(d, q)) if d == 0 else zmod(z + out_dist(d, q))

    def out_send(a, d, zz, column, slot):
        ref = out_part(a, zz, c, column)
        target = zmod(z + 1) if d == 0 else zmod(z - 1)
        return remote(ref, ref, os_.at[d], orr.at[a, d, slot], dev(target, c, h))

    def out_to_sib(a, d, zz, column, slot):
        ref = out_part(a, zz, c, column)
        return remote(ref, ref, ws.at[0], wr.at[0], sib)

    def next_slot(d, q):
        return jnp.where(near[d] < 4, q, q + 4)

    def serve_out(t):
        if t == 0:

            @pl.when(is_source)
            def _():
                got_all(cr.at[0], w_out.at[pl.ds(0, 96), :])

        if t < 4:

            @pl.when(is_source)
            def _():
                for a in (0, 1):
                    for d in (0, 1):
                        out_send(a, d, z, t, t).start()
                    out_to_sib(a, 2, z, t, t).start()

        if t > 0:
            for a in (0, 1):
                for d in (0, 1):
                    q = t - near[d]
                    reach = out_dist(d, q)

                    @pl.when((q >= 0) & (q < 8) & (reach <= OUT_FAR[a][d]))
                    def _():
                        zz, column = out_origin(d, q), q % 4
                        out_send(a, d, zz, column, q).wait_recv()

                        @pl.when(reach < OUT_FAR[a][d])
                        def _():
                            out_send(a, d, zz, column, next_slot(d, q)).start()

                        out_to_sib(a, d, zz, column, q).start()

    def out_end():
        got_all(wr.at[0], w_out.at[pl.ds(0, 512), :])

    def out_drain():
        for d in (0, 1):

            @pl.when(near[d] == 3)
            def _():
                sent_all(os_.at[d], w_out.at[pl.ds(0, 192), :])

            @pl.when(near[d] != 3)
            def _():
                sent_all(os_.at[d], w_out.at[pl.ds(0, 256), :])

        sent_all(ws.at[0], w_out.at[pl.ds(0, 512), :])

        @pl.when(jnp.logical_not(is_source))
        def _():
            sent_all(cs.at[0], land)

    def hand_on(p, d, k):
        to_sib(p, d, k).start()

    def first(p):
        ring(p, 0, 0, 1).start()
        ring(p, 1, 0, 1).start()
        hand_on(p, 0, 0)

    def event(p, d, k, forward):
        ring(p, d, k, k).wait_recv()
        if forward:
            ring(p, d, k, k + 1).start()
        hand_on(p, d, k)

    def columns(zz):
        return pl.ds(pl.multiple_of(zz * 256, 256), 256)

    def dots_in(*planes):
        acc_i[...] += sum(
            jnp.dot(act[:, columns(zz)], w_in[columns(zz), :], preferred_element_type=F32)
            for zz in planes
        )

    def dots_gs(*planes):
        acc_s[...] += sum(
            lax.dot_general(
                act[:, columns(zz)],
                w_gs[:, columns(zz)],
                (((1,), (1,)), ((), ())),
                preferred_element_type=F32,
            )
            for zz in planes
        )

    first(0)
    load_in.wait()
    first(1)
    first(2)
    send_halo.start()
    load_gate.wait()
    first(3)
    first(4)
    scaled = (wo_ref[...].astype(F32) * gain_ref[...]).astype(BF16)

    @pl.when(is_source)
    def _():
        w_out[pl.ds(out_rows(z, c), 128), pl.ds(pl.multiple_of(256 * y, 256), 256)] = scaled

    @pl.when(jnp.logical_not(is_source))
    def _():
        land[...] = scaled
        bring(y).start()

    acc_i[...] = jnp.zeros_like(acc_i)
    acc_s[...] = jnp.zeros_like(acc_s)

    def serve(pieces, k):
        for p in pieces:
            for d in (0, 1):
                if k <= FAR[p][d]:
                    event(p, d, k, k < FAR[p][d])

    def use(kind, dots, k):
        from_sib(kind, 0, k)
        if k == 8:
            dots(origin(0, k))
        else:
            from_sib(kind, 1, k)
            dots(origin(0, k), origin(1, k))

    IN = (1, 2)
    GATE = (3, 4)

    serve((0,), 1)
    serve(IN, 1)
    load_act.wait()
    send_halo.wait()
    for kind in (0, 1):
        from_sib(kind, 0, 0)
    dots_gs(z)
    dots_in(z)
    for k in (2, 3, 4, 5, 6, 7):
        serve((0, 1), k)
        use(0, dots_gs, k - 1)
        serve((2,), k)
        use(1, dots_in, k - 1)
        serve(GATE, k - 1)
    serve_out(0)
    serve((0,), 8)
    use(0, dots_gs, 7)
    use(0, dots_gs, 8)
    serve_out(1)

    not_first = jnp.where(s == 0, 0.0, 1.0).astype(F32)
    lane128 = lax.broadcasted_iota(jnp.int32, (TOK, 128), 1)
    raw = acc_s[HALO:, :]
    acc_s[...] = acc_s[...].astype(BF16).astype(F32)
    acc_s[0:HALO, :] = acc_s[0:HALO, :] * not_first
    tap_tile = tapg_ref[...]
    tap_g = jnp.where(y % 2 == 0, tap_tile, pltpu.roll(tap_tile, 64, axis=1))
    conv = jnp.zeros((TOK, 80), F32)
    for position in range(4):
        conv = conv + acc_s[pl.ds(HALO - 3 + position, TOK), :] * tap_g[position : position + 1, :80]
    conv = conv * jax.nn.sigmoid(conv)
    both = jnp.where(lane128[:, :80] < 64, conv, raw)
    both_t = jnp.concatenate([both, jnp.zeros((TOK, 48), F32)], axis=1).T
    own_cols = pl.ds(pl.multiple_of(64 * y, 64), 64)
    bct[own_cols, :] = both_t[0:64].astype(BF16)

    def y_copy(j, where):
        rows = bct.at[pl.ds(pl.multiple_of(64 * where, 64), 64), :]
        return remote(rows, rows, ys.at[0], yr.at[0], dev(z, c, hid_at(0, j)))

    for j in (1, 3, 2):
        y_copy(j, y).start()

    serve(IN, 8)
    serve(GATE, 7)
    use(1, dots_in, 7)

    step4 = jnp.where(
        y < 2,
        jnp.where(y == 0, both_t[64:68], both_t[68:72]),
        jnp.where(y == 2, both_t[72:76], both_t[76:80]),
    )
    step8 = jnp.concatenate([step4, step4], axis=0)
    head = lax.broadcasted_iota(jnp.int32, (8, TOK), 0) % 4
    lane = lax.broadcasted_iota(jnp.int32, (8, TOK), 1)

    def per_head(ref):
        return jnp.where(
            head < 2, jnp.where(head == 0, ref[0], ref[1]), jnp.where(head == 2, ref[2], ref[3])
        )

    v = step8 + per_head(bias_ref)
    dt = jnp.maximum(v, 0.0) + jnp.log1p(jnp.exp(-jnp.abs(v)))
    cum = dt * -jnp.exp(per_head(decay_ref))
    for shift in (1, 2, 4, 8, 16, 32, 64, 128):
        cum = cum + jnp.where(lane % 256 >= shift, pltpu.roll(cum, shift, axis=1), 0.0)
    last = jnp.where(lane < 256, cum[:, 255:256], cum[:, 511:512])
    weight = jnp.exp(last - cum) * dt
    stack = jnp.concatenate([cum, weight, jnp.exp(cum), jnp.zeros((104, TOK), F32)], axis=0)
    cols[...] = stack.T

    def expand(q):
        halves = []
        for i in (0, 2):
            lo = jnp.broadcast_to(cols[:, 8 * q + i : 8 * q + i + 1], (TOK, 128))
            hi = jnp.broadcast_to(cols[:, 8 * q + i + 1 : 8 * q + i + 2], (TOK, 128))
            halves.append(jnp.where(lane128 < 64, lo, hi))
        return jnp.concatenate(halves, axis=1)

    use(1, dots_in, 8)
    serve_out(2)
    acc_i[...] = acc_i[...].astype(BF16).astype(F32)
    acc_i[0:HALO, :] = acc_i[0:HALO, :] * not_first
    conv = jnp.zeros((TOK, 256), F32)
    for position in range(4):
        conv = conv + acc_i[pl.ds(HALO - 3 + position, TOK), :] * tapi_ref[position : position + 1, :]
    conv = conv * jax.nn.sigmoid(conv)
    xc[...] = conv.astype(BF16)

    head_lane = lax.broadcasted_iota(jnp.int32, (1, 256), 1) // 64
    weighted = (xc[...].astype(F32) * expand(1)).astype(BF16)
    expcum = expand(2)
    decay0 = expcum[255:256]
    decay1 = expcum[511:512]

    serve_out(3)
    got_all(yr.at[0], bct.at[pl.ds(0, 192), :])
    fresh0 = jnp.dot(bct[0:128, 0:256], weighted[0:256], preferred_element_type=F32)
    fresh1 = jnp.dot(bct[0:128, 256:512], weighted[256:512], preferred_element_type=F32)
    end_own = decay1 * fresh0 + fresh1
    total_own = decay0 * decay1
    th, tl = split(jnp.broadcast_to(total_own, (8, 256)))
    tail = jnp.concatenate([th.astype(F32), tl.astype(F32)], axis=0).astype(BF16)
    e_own[0:128, :] = end_own.astype(BF16)
    e_own[128:144, :] = tail
    swap = remote(e_own, e_sib, es.at[0], es.at[1], sib)
    swap.start()

    serve(GATE, 8)
    swap.wait()

    end_sib = e_sib[0:128, :].astype(F32)
    total_sib = e_sib[128:129, :].astype(F32) + e_sib[136:137, :].astype(F32)

    def my_half(value):
        return jnp.where(c == 0, value[:, 0:128], value[:, 128:256])

    second_decay = jnp.where(c == 0, total_sib, total_own)
    chip_end = second_decay * jnp.where(c == 0, end_own, end_sib) + jnp.where(
        c == 0, end_sib, end_own
    )
    chip_total = jnp.broadcast_to(my_half(total_own * total_sib), (8, 128))
    th, tl = split(chip_total)
    tbuf[z, 0:128, :] = my_half(chip_end).astype(BF16)
    tbuf[z, 128:144, :] = jnp.concatenate([th.astype(F32), tl.astype(F32)], axis=0).astype(BF16)

    def t_send(d, k, hop):
        ref = tbuf.at[origin(d, k)]
        target = zmod(z + hop) if d == 0 else zmod(z - hop)
        return remote(ref, ref, ts.at[0], tr.at[d, k + hop - 1], dev(target, c, h))

    def t_recv(d, k):
        ref = tbuf.at[origin(d, k)]
        got_all(tr.at[d, k - 1], ref)

    def t_start(d, k, hop):
        t_send(d, k, hop).start()

    for hop in (2, 1):
        for d in (0, 1):
            t_start(d, 0, hop)

    serve_out(4)

    row = lax.broadcasted_iota(jnp.int32, (256, 256), 0)
    column = lax.broadcasted_iota(jnp.int32, (256, 256), 1)
    c_mat = bct[128:256, :].astype(F32).T.astype(BF16)
    intra = []

    def span(q):
        tokens = slice(256 * q, 256 * q + 256)
        scores = jnp.dot(c_mat[tokens], bct[0:128, tokens], preferred_element_type=F32)
        scores = jnp.where(row >= column, scores, 0.0)
        total = jnp.zeros((256, 256), F32)
        for i in range(4):
            gap = jnp.minimum(cols[tokens, i : i + 1] - cum[i : i + 1, tokens], 0.0)
            mixing = (scores * jnp.exp(gap) * dt[i : i + 1, tokens]).astype(BF16)
            x_head = jnp.where(head_lane == i, xc[tokens, :].astype(F32), 0.0).astype(BF16)
            total = total + jnp.dot(mixing, x_head, preferred_element_type=F32)
        return total

    mixed0 = span(0)

    def gate_half(q):
        tokens = slice(256 * q, 256 * q + 256)
        acc_g[tokens, :] = jnp.dot(
            act[HALO + 256 * q : HALO + 256 * q + 256, :], w_gate[...], preferred_element_type=F32
        )

    got_all(br_gate.at[0], w_gate.at[pl.ds(0, 2048), :])
    gate_half(0)
    for d in (0, 1):
        t_recv(d, 2)
        for hop in (2, 1):
            t_start(d, 2, hop)
    serve_out(5)
    mixed1 = span(1)
    gate_half(1)
    skip = jnp.where(
        head_lane < 2,
        jnp.where(head_lane == 0, skip_ref[0], skip_ref[1]),
        jnp.where(head_lane == 2, skip_ref[2], skip_ref[3]),
    )
    xf = xc[...].astype(F32)
    mixed0 = mixed0 + skip * xf[0:256]
    mixed1 = mixed1 + skip * xf[256:512]
    for d in (0, 1):
        t_recv(d, 4)
        for hop in (2, 1):
            t_start(d, 4, hop)
    serve_out(6)
    t_recv(0, 6)
    for hop in (2, 1):
        t_start(0, 6, hop)
    t_recv(1, 6)
    t_start(1, 6, 1)
    serve_out(7)
    for d, ks in ((0, (1, 3, 5, 7, 8)), (1, (1, 3, 5, 7))):
        for k in ks:
            t_recv(d, k)

    prefix = jnp.zeros((128, 128), F32)
    for k in range(15, 0, -1):
        zz = zmod(z - k)
        decay = tbuf[zz, 128:129, :].astype(F32) + tbuf[zz, 136:137, :].astype(F32)
        joined = decay * prefix + tbuf[zz, 0:128, :].astype(F32)
        prefix = jnp.where(z >= k, joined, prefix)
    pbuf[...] = prefix
    swap2 = remote(pbuf, psib, es.at[2], es.at[3], sib)
    swap2.start()
    serve_out(8)
    swap2.wait()
    other = psib[...]
    before = jnp.where(
        c == 0,
        jnp.concatenate([prefix, other], axis=1),
        jnp.concatenate([other, prefix], axis=1),
    )
    state0 = jnp.where(c == 0, before, total_sib * before + end_sib)
    state1 = decay0 * state0 + fresh0

    def gated(q, mixed, state):
        tokens = slice(256 * q, 256 * q + 256)
        high, low = split(state)
        inter = jnp.dot(c_mat[tokens], high, preferred_element_type=F32)
        inter = inter + jnp.dot(c_mat[tokens], low, preferred_element_type=F32)
        mixed = mixed + inter * expcum[tokens]
        gate = acc_g[tokens, :].astype(BF16).astype(F32)
        gath[tokens, pl.ds(pl.multiple_of(256 * y, 256), 256)] = (
            mixed * (gate * jax.nn.sigmoid(gate))
        ).astype(BF16)

    def part(u, a, first_row, rows):
        column = pl.multiple_of(256 * lax.rem(y + a + 4, 4), 256)
        return gath.at[pl.ds(128 * u + first_row, rows), pl.ds(column, 256)]

    STEP = (1, -1)

    def g_near(u, way, a):
        ref = part(u, a, 0, 128)
        return remote(ref, ref, gs.at[0], gr.at[u, way], dev(z, c, hid_at(0, STEP[way])))

    def g_far(u, way, a):
        ref = part(u, a, 64 * way, 64)
        return remote(
            ref, ref, gs.at[0], gr.at[u, 2], dev(z, c, hid_at(0, STEP[way]))
        )

    def near_start(u):
        for way in (0, 1):
            g_near(u, way, 0).start()

    def near_take(u):
        for way in (0, 1):
            g_near(u, way, -STEP[way]).wait_recv()
            g_far(u, way, -STEP[way]).start()

    gated(0, mixed0, state0)
    near_start(0)
    near_start(1)
    gated(1, mixed1, state1)
    near_start(2)
    serve_out(9)

    def drain_weights():
        sent_all(zs.at[0], w_gs.at[:, pl.ds(0, 1920)])
        sent_all(bs.at[0], w_gs.at[:, pl.ds(0, 2048)])
        for kind, ref in ((1, w_in), (2, w_gate)):
            sent_all(zs.at[kind], ref.at[pl.ds(0, 1920), :])
            sent_all(bs.at[kind], ref.at[pl.ds(0, 2048), :])

    near_take(0)
    near_take(1)
    near_start(3)
    serve_out(10)
    near_take(2)
    serve_out(11)
    near_take(3)
    out_end()

    def product(u, offset):
        rows = pl.ds(pl.multiple_of(256 * lax.rem(x + offset, 4), 256), 256)
        return lax.dot_general(
            gath[256 * u : 256 * u + 256, :],
            w_out[rows, :],
            (((1,), (1,)), ((), ())),
            preferred_element_type=F32,
        )

    def along(u, slot, way, src, dst):
        landed = hr.at[u, way if slot == 0 else 2]
        return remote(src, dst, hs.at[0], landed, dev(z, c, hid_at(STEP[way], 0)))

    top = pl.ds(0, 128)
    low = pl.ds(128, 128)

    def far_send(u, way):
        return along(u, 0, way, s_far.at[u, (top, low)[way]], (r_up, r_down)[way].at[u])

    def early_send(u, way):
        rows = (low, top)[way]
        return along(u, 1, way, (s_up, s_down)[way].at[u, rows], (f_up, f_down)[way].at[u, rows])

    def late_send(u, way):
        rows = (top, low)[way]
        return along(u, 2, way, (s_up, s_down)[way].at[u, rows], (f_up, f_down)[way].at[u, rows])

    def square_send(u, j):
        return remote(
            sq_own.at[u], sq_in.at[u, j - 1], qs.at[0], qr.at[u], dev(z, c, hid_at(j, 0))
        )

    def multiply_far(u):
        s_far[u] = product(u, 2).astype(BF16)
        for way in (0, 1):
            far_send(u, way).start()

    def multiply_near(u):
        up = product(u, 1)
        s_up[u, 128:256, :] = up[128:256].astype(BF16)
        early_send(u, 0).start()
        p_up[u] = up[0:128]
        down = product(u, 3)
        s_down[u, 0:128, :] = down[0:128].astype(BF16)
        early_send(u, 1).start()
        p_down[u] = down[128:256]

    def square(u):
        total = jnp.zeros((256, 128), F32)
        for i in range(8):
            g = gath[256 * u : 256 * u + 256, 128 * i : 128 * i + 128].astype(F32)
            total = total + g * g
        sq_own[u] = jnp.broadcast_to(jnp.sum(total.T, axis=0, keepdims=True), (8, 256))
        for j in (1, 3, 2):
            square_send(u, j).start()

    def add(u):
        far_send(u, 0).wait_recv()
        s_up[u, 0:128, :] = (p_up[u] + r_up[u].astype(F32)).astype(BF16)
        late_send(u, 0).start()
        far_send(u, 1).wait_recv()
        s_down[u, 128:256, :] = (p_down[u] + r_down[u].astype(F32)).astype(BF16)
        late_send(u, 1).start()

    def finish(u):
        got_all(qr.at[u], sq_in.at[u])
        squares = sq_own[u] + sq_in[u, 0] + sq_in[u, 1] + sq_in[u, 2]
        scale = lax.rsqrt(squares / INNER + 1e-5)
        scale = jnp.broadcast_to(scale[0:1], (128, 256)).T
        got_all(hr.at[u, 2], gath.at[pl.ds(0, 128), :])
        value = p_own[u] + f_up[u].astype(F32) + f_down[u].astype(F32)
        for half_of in (0, 128):
            out_ref[256 * u : 256 * u + 256, half_of : half_of + 128] = (
                value[:, half_of : half_of + 128] * scale
            ).astype(BF16)

    for u in range(4):
        got_all(gr.at[u, 2], part(u, 2, 0, 128))
        if u % 2 == 1:
            multiply_far(u // 2)
            multiply_near(u // 2)
    square(0)
    add(0)
    p_own[0] = product(0, 0)
    square(1)
    add(1)
    p_own[1] = product(1, 0)
    drain_weights()
    out_drain()
    sent_all(ys.at[0], bct.at[pl.ds(0, 192), :])
    sent_all(ts.at[0], tbuf.at[pl.ds(0, 15)])
    finish(0)
    finish(1)
    sent_all(gs.at[0], gath.at[pl.ds(0, 384), :])
    sent_all(hs.at[0], gath.at[pl.ds(0, 384), :])
    sent_all(qs.at[0], sq_in)


def local(
    activations,
    w_inner,
    w_gate,
    w_groups,
    w_step,
    w_out,
    conv_inner,
    conv_groups,
    step_bias,
    decay_log,
    skip_gain,
    norm_gain,
):
    anywhere = pl.BlockSpec(memory_space=pl.ANY)
    vmem = pl.BlockSpec(memory_space=pltpu.VMEM)
    dma = pltpu.SemaphoreType.DMA
    return pl.pallas_call(
        kernel,
        out_shape=jax.ShapeDtypeStruct((TOK, 256), BF16),
        in_specs=[anywhere] * 12,
        out_specs=vmem,
        scratch_shapes=[
            pltpu.VMEM((128, 256), BF16),
            pltpu.VMEM((128, 128), BF16),
            pltpu.VMEM((64, 128), BF16),
            pltpu.VMEM((4, 256), F32),
            pltpu.VMEM((4, 128), F32),
            pltpu.SMEM((4,), F32),
            pltpu.SMEM((4,), F32),
            pltpu.SMEM((4,), F32),
            pltpu.VMEM((1, 256), F32),
            dma((9,)),
            pltpu.VMEM((HALO + TOK, 4096), BF16),
            pltpu.VMEM((4096, 256), BF16),
            pltpu.VMEM((4096, 256), BF16),
            pltpu.VMEM((80, 4096), BF16),
            pltpu.VMEM((128, 256), BF16),
            pltpu.VMEM((1024, 1024), BF16),
            pltpu.VMEM((TOK, 1024), BF16),
            pltpu.VMEM((2, 8, 256), F32),
            pltpu.VMEM((2, 3, 8, 256), F32),
            pltpu.VMEM((2, 128, 256), F32),
            pltpu.VMEM((2, 128, 256), F32),
            pltpu.VMEM((2, 256, 256), F32),
            pltpu.VMEM((2, 256, 256), BF16),
            pltpu.VMEM((2, 256, 256), BF16),
            pltpu.VMEM((2, 256, 256), BF16),
            pltpu.VMEM((2, 128, 256), BF16),
            pltpu.VMEM((2, 128, 256), BF16),
            pltpu.VMEM((2, 256, 256), BF16),
            pltpu.VMEM((2, 256, 256), BF16),
            pltpu.VMEM((HALO + TOK, 256), F32),
            pltpu.VMEM((TOK, 256), F32),
            pltpu.VMEM((HALO + TOK, 80), F32),
            pltpu.VMEM((256, TOK), BF16),
            pltpu.VMEM((TOK, 256), BF16),
            pltpu.VMEM((TOK, 128), F32),
            pltpu.VMEM((144, 256), BF16),
            pltpu.VMEM((144, 256), BF16),
            pltpu.VMEM((16, 144, 128), BF16),
            pltpu.VMEM((128, 128), F32),
            pltpu.VMEM((128, 128), F32),
            dma((3,)),
            dma((2,)),
            dma((3,)),
            dma((5, 2, 8)),
            dma((3,)),
            dma((2, 2, 9)),
            dma((1,)),
            dma((1,)),
            dma((1,)),
            dma((2,)),
            dma((2, 2, 8)),
            dma((1,)),
            dma((1,)),
            dma((1,)),
            dma((1,)),
            dma((4,)),
            dma((1,)),
            dma((2, 8)),
            dma((1,)),
            dma((4, 3)),
            dma((1,)),
            dma((2,)),
            dma((1,)),
            dma((2, 3)),
        ],
        compiler_params=pltpu.CompilerParams(
            collective_id=0, has_side_effects=True, vmem_limit_bytes=67043328
        ),
    )(
        activations,
        w_inner,
        w_gate,
        w_out,
        w_groups,
        w_step.T,
        conv_inner,
        conv_groups,
        step_bias,
        decay_log,
        skip_gain,
        norm_gain.reshape(1, 256),
    )


def solution(mesh):
    in_specs = (
        P("seq", None),
        P("seq", "hid"),
        P("seq", "hid"),
        P("seq", None),
        P("seq", None),
        P("seq", "hid"),
        P(None, "hid"),
        P(),
        P("hid"),
        P("hid"),
        P("hid"),
        P("hid"),
    )
    return jax.shard_map(
        local, mesh=mesh, in_specs=in_specs, out_specs=P("seq", "hid"), check_vma=False
    )
```

```python
import jax
import jax.numpy as jnp
from jax import lax
from jax.experimental import pallas as pl
from jax.experimental.pallas import tpu as pltpu
from jax.sharding import PartitionSpec as P

F32 = jnp.float32
BF16 = jnp.bfloat16
MESH = pl.DeviceIdType.MESH
INNER = 4096
TOK = 512
HALO = 8
NZ = 16
FAR = ((8, 7), (8, 7), (7, 8), (8, 7), (7, 8))
KIND = (0, 1, 1, 2, 2)


def remote(src, dst, send, recv, device):
    return pltpu.make_async_remote_copy(
        src_ref=src, dst_ref=dst, send_sem=send, recv_sem=recv, device_id=device, device_id_type=MESH
    )


def split(value):
    high = value.astype(BF16)
    return high, (value - high.astype(F32)).astype(BF16)


def kernel(
    act_hbm,
    wi_hbm,
    wg_hbm,
    wo_hbm,
    wgr_hbm,
    wst_hbm,
    tapi_hbm,
    tapg_hbm,
    bias_hbm,
    decay_hbm,
    skip_hbm,
    gain_hbm,
    out_ref,
    wo_ref,
    wgr_ref,
    wst_ref,
    tapi_ref,
    tapg_ref,
    bias_ref,
    decay_ref,
    skip_ref,
    gain_ref,
    small_sem,
    act,
    w_in,
    w_gate,
    w_gs,
    land,
    w_out,
    gath,
    sq_own,
    sq_in,
    p_up,
    p_down,
    p_own,
    s_far,
    s_up,
    s_down,
    r_up,
    r_down,
    f_up,
    f_down,
    acc_i,
    acc_g,
    acc_s,
    bct,
    xc,
    cols,
    e_own,
    e_sib,
    tbuf,
    pbuf,
    psib,
    local_sem,
    halo_sem,
    zs,
    zr,
    bs,
    br,
    br_gate,
    cs,
    cr,
    os_,
    orr,
    ws,
    wr,
    ys,
    yr,
    es,
    ts,
    tr,
    gs,
    gr,
    qs,
    qr,
    hs,
    hr,
):
    s = lax.axis_index("seq")
    h = lax.axis_index("hid")
    z = s // 2
    c = s % 2
    x = h // 4
    y = h % 4

    def dev(zz, cc, hh):
        return {"seq": 2 * zz + cc, "hid": hh}

    def zmod(v):
        return lax.rem(v + 2 * NZ, NZ)

    def hid_at(dx, dy):
        return lax.rem(x + dx + 4, 4) * 4 + lax.rem(y + dy + 4, 4)

    sib = dev(z, 1 - c, h)
    after = {"seq": lax.rem(s + 1, 32), "hid": h}
    extra = {"seq": lax.rem(s + 2 * c - 1 + 32, 32), "hid": h}

    load_act = pltpu.make_async_copy(act_hbm, act.at[pl.ds(HALO, TOK), :], local_sem.at[0])
    own_rows = pl.ds(pl.multiple_of(s * 128, 128), 128)
    load_in = pltpu.make_async_copy(wi_hbm, w_in.at[own_rows, :], local_sem.at[1])
    load_gate = pltpu.make_async_copy(wg_hbm, w_gate.at[own_rows, :], local_sem.at[2])
    group_cols = pl.ds(pl.multiple_of(x * 256 + (y // 2) * 128, 128), 128)
    small = [
        pltpu.make_async_copy(src, dst, small_sem.at[i])
        for i, (src, dst) in enumerate(
            (
                (wgr_hbm.at[:, group_cols], wgr_ref),
                (wst_hbm, wst_ref),
                (wo_hbm, wo_ref),
                (gain_hbm, gain_ref),
                (tapi_hbm, tapi_ref),
                (tapg_hbm.at[:, group_cols], tapg_ref),
                (bias_hbm, bias_ref),
                (decay_hbm, decay_ref),
                (skip_hbm, skip_ref),
            )
        )
    ]
    load_in.start()
    for item in small:
        item.start()
    load_gate.start()
    load_act.start()

    barrier = pltpu.get_barrier_semaphore()
    for step in (1, -1, 2, -2):
        pl.semaphore_signal(barrier, inc=1, device_id=dev(zmod(z + step), c, h), device_id_type=MESH)
    pl.semaphore_signal(barrier, inc=1, device_id=sib, device_id_type=MESH)
    pl.semaphore_signal(barrier, inc=1, device_id=extra, device_id_type=MESH)
    for step in (1, 2, 3):
        for hh in (hid_at(step, 0), hid_at(0, step)):
            pl.semaphore_signal(barrier, inc=1, device_id=dev(z, c, hh), device_id_type=MESH)

    for item in small:
        item.wait()
    tile = wgr_ref[...].astype(F32).T
    half = jnp.where(y % 2 == 0, tile[:64], tile[64:])
    steps_t = wst_ref[...].astype(F32)
    mine = jnp.where(
        x < 2,
        jnp.where(x == 0, steps_t[0:16], steps_t[16:32]),
        jnp.where(x == 2, steps_t[32:48], steps_t[48:64]),
    )
    own_lanes = pl.ds(pl.multiple_of(s * 128, 128), 128)
    w_gs[0:64, own_lanes] = half.astype(BF16)
    w_gs[64:80, own_lanes] = mine.astype(BF16)

    pl.semaphore_wait(barrier, 12)

    send_halo = remote(
        act_hbm.at[pl.ds(TOK - HALO, HALO), :],
        act.at[pl.ds(0, HALO), :],
        halo_sem.at[0],
        halo_sem.at[1],
        after,
    )

    def sent_all(sem, ref):
        remote(ref, ref, sem, sem, sib).wait_send()

    def got_all(sem, ref):
        remote(ref, ref, sem, sem, sib).wait_recv()

    def block(p, zz):
        row = pl.multiple_of((2 * zz + c) * 128, 128)
        if p == 0:
            return w_gs.at[:, pl.ds(row, 128)]
        part = 64 * ((p - 1) % 2)
        if p < 3:
            return w_in.at[pl.ds(row + part, 64), :]
        return w_gate.at[pl.ds(row + part, 64), :]

    def sib_block(kind, zz):
        row = pl.multiple_of((2 * zz + 1 - c) * 128, 128)
        if kind == 0:
            return w_gs.at[:, pl.ds(row, 128)]
        return w_in.at[pl.ds(row, 128), :]

    def origin(d, k):
        return zmod(z - k) if d == 0 else zmod(z + k)

    def ring(p, d, k, recv_k):
        ref = block(p, origin(d, k))
        target = zmod(z + 1) if d == 0 else zmod(z - 1)
        return remote(ref, ref, zs.at[KIND[p]], zr.at[p, d, recv_k - 1], dev(target, c, h))

    def to_sib(p, d, k):
        ref = block(p, origin(d, k))
        kind = KIND[p]
        landed = br_gate.at[0] if kind == 2 else br.at[kind, 0 if k == 8 else d, k]
        return remote(ref, ref, bs.at[kind], landed, sib)

    def from_sib(kind, d, k):
        got_all(br.at[kind, d, k], sib_block(kind, origin(d, k)))

    keeper = z % 4
    is_source = keeper == y

    def out_rows(zz, cc):
        return pl.multiple_of((zz // 4) * 256 + 128 * cc, 128)

    def out_part(a, zz, cc, column):
        return w_out.at[
            pl.ds(out_rows(zz, cc) + 64 * a, 64), pl.ds(pl.multiple_of(256 * column, 256), 256)
        ]

    def bring(column):
        return remote(
            land,
            w_out.at[pl.ds(out_rows(z, c), 128), pl.ds(pl.multiple_of(256 * column, 256), 256)],
            cs.at[0],
            cr.at[0],
            dev(z, c, x * 4 + keeper),
        )

    near = tuple((d + 3) % 4 + 1 for d in (z - y + 16, y - z + 16))
    OUT_FAR = ((8, 7), (7, 8))

    def out_dist(d, q):
        return near[d] + 4 * (q // 4)

    def out_origin(d, q):
        return zmod(z - out_dist(d, q)) if d == 0 else zmod(z + out_dist(d, q))

    def out_send(a, d, zz, column, slot):
        ref = out_part(a, zz, c, column)
        target = zmod(z + 1) if d == 0 else zmod(z - 1)
        return remote(ref, ref, os_.at[d], orr.at[a, d, slot], dev(target, c, h))

    def out_to_sib(a, d, zz, column, slot):
        ref = out_part(a, zz, c, column)
        return remote(ref, ref, ws.at[0], wr.at[0], sib)

    def next_slot(d, q):
        return jnp.where(near[d] < 4, q, q + 4)

    def serve_out(t):
        if t == 0:

            @pl.when(is_source)
            def _():
                got_all(cr.at[0], w_out.at[pl.ds(0, 96), :])

        if t < 4:

            @pl.when(is_source)
            def _():
                for a in (0, 1):
                    for d in (0, 1):
                        out_send(a, d, z, t, t).start()
                    out_to_sib(a, 2, z, t, t).start()

        if t > 0:
            for a in (0, 1):
                for d in (0, 1):
                    q = t - near[d]
                    reach = out_dist(d, q)

                    @pl.when((q >= 0) & (q < 8) & (reach <= OUT_FAR[a][d]))
                    def _():
                        zz, column = out_origin(d, q), q % 4
                        out_send(a, d, zz, column, q).wait_recv()

                        @pl.when(reach < OUT_FAR[a][d])
                        def _():
                            out_send(a, d, zz, column, next_slot(d, q)).start()

                        out_to_sib(a, d, zz, column, q).start()

    def out_end():
        got_all(wr.at[0], w_out.at[pl.ds(0, 512), :])

    def out_drain():
        for d in (0, 1):

            @pl.when(near[d] == 3)
            def _():
                sent_all(os_.at[d], w_out.at[pl.ds(0, 192), :])

            @pl.when(near[d] != 3)
            def _():
                sent_all(os_.at[d], w_out.at[pl.ds(0, 256), :])

        sent_all(ws.at[0], w_out.at[pl.ds(0, 512), :])

        @pl.when(jnp.logical_not(is_source))
        def _():
            sent_all(cs.at[0], land)

    def hand_on(p, d, k):
        to_sib(p, d, k).start()

    def first(p):
        ring(p, 0, 0, 1).start()
        ring(p, 1, 0, 1).start()
        hand_on(p, 0, 0)

    def event(p, d, k, forward):
        ring(p, d, k, k).wait_recv()
        if forward:
            ring(p, d, k, k + 1).start()
        hand_on(p, d, k)

    def columns(zz):
        return pl.ds(pl.multiple_of(zz * 256, 256), 256)

    def dots_in(*planes):
        acc_i[...] += sum(
            jnp.dot(act[:, columns(zz)], w_in[columns(zz), :], preferred_element_type=F32)
            for zz in planes
        )

    def dots_gs(*planes):
        acc_s[...] += sum(
            lax.dot_general(
                act[:, columns(zz)],
                w_gs[:, columns(zz)],
                (((1,), (1,)), ((), ())),
                preferred_element_type=F32,
            )
            for zz in planes
        )

    first(0)
    load_in.wait()
    first(1)
    first(2)
    send_halo.start()
    load_gate.wait()
    first(3)
    first(4)
    scaled = (wo_ref[...].astype(F32) * gain_ref[...]).astype(BF16)

    @pl.when(is_source)
    def _():
        w_out[pl.ds(out_rows(z, c), 128), pl.ds(pl.multiple_of(256 * y, 256), 256)] = scaled

    @pl.when(jnp.logical_not(is_source))
    def _():
        land[...] = scaled
        bring(y).start()

    acc_i[...] = jnp.zeros_like(acc_i)
    acc_s[...] = jnp.zeros_like(acc_s)

    def serve(pieces, k):
        for p in pieces:
            for d in (0, 1):
                if k <= FAR[p][d]:
                    event(p, d, k, k < FAR[p][d])

    def use(kind, dots, k):
        from_sib(kind, 0, k)
        if k == 8:
            dots(origin(0, k))
        else:
            from_sib(kind, 1, k)
            dots(origin(0, k), origin(1, k))

    IN = (1, 2)
    GATE = (3, 4)

    serve((0,), 1)
    serve(IN, 1)
    load_act.wait()
    send_halo.wait()
    for kind in (0, 1):
        from_sib(kind, 0, 0)
    dots_gs(z)
    dots_in(z)
    for k in (2, 3, 4, 5, 6, 7):
        serve((0, 1), k)
        use(0, dots_gs, k - 1)
        serve((2,), k)
        serve((3,), k - 1)
        use(1, dots_in, k - 1)
        serve((4,), k - 1)
    serve_out(0)
    serve((0,), 8)
    use(0, dots_gs, 7)
    use(0, dots_gs, 8)
    serve_out(1)

    not_first = jnp.where(s == 0, 0.0, 1.0).astype(F32)
    lane128 = lax.broadcasted_iota(jnp.int32, (TOK, 128), 1)
    raw = acc_s[HALO:, :]
    acc_s[...] = acc_s[...].astype(BF16).astype(F32)
    acc_s[0:HALO, :] = acc_s[0:HALO, :] * not_first
    tap_tile = tapg_ref[...]
    tap_g = jnp.where(y % 2 == 0, tap_tile, pltpu.roll(tap_tile, 64, axis=1))
    conv = jnp.zeros((TOK, 80), F32)
    for position in range(4):
        conv = conv + acc_s[pl.ds(HALO - 3 + position, TOK), :] * tap_g[position : position + 1, :80]
    conv = conv * jax.nn.sigmoid(conv)
    both = jnp.where(lane128[:, :80] < 64, conv, raw)
    both_t = jnp.concatenate([both, jnp.zeros((TOK, 48), F32)], axis=1).T
    own_cols = pl.ds(pl.multiple_of(64 * y, 64), 64)
    bct[own_cols, :] = both_t[0:64].astype(BF16)

    def y_copy(j, where):
        rows = bct.at[pl.ds(pl.multiple_of(64 * where, 64), 64), :]
        return remote(rows, rows, ys.at[0], yr.at[0], dev(z, c, hid_at(0, j)))

    for j in (1, 3, 2):
        y_copy(j, y).start()

    step4 = jnp.where(
        y < 2,
        jnp.where(y == 0, both_t[64:68], both_t[68:72]),
        jnp.where(y == 2, both_t[72:76], both_t[76:80]),
    )
    step8 = jnp.concatenate([step4, step4], axis=0)
    head = lax.broadcasted_iota(jnp.int32, (8, TOK), 0) % 4
    lane = lax.broadcasted_iota(jnp.int32, (8, TOK), 1)

    def per_head(ref):
        return jnp.where(
            head < 2, jnp.where(head == 0, ref[0], ref[1]), jnp.where(head == 2, ref[2], ref[3])
        )

    v = step8 + per_head(bias_ref)
    dt = jnp.maximum(v, 0.0) + jnp.log1p(jnp.exp(-jnp.abs(v)))
    cum = dt * -jnp.exp(per_head(decay_ref))
    for shift in (1, 2, 4, 8, 16, 32, 64, 128):
        cum = cum + jnp.where(lane % 256 >= shift, pltpu.roll(cum, shift, axis=1), 0.0)
    last = jnp.where(lane < 256, cum[:, 255:256], cum[:, 511:512])
    weight = jnp.exp(last - cum) * dt
    stack = jnp.concatenate([cum, weight, jnp.exp(cum), jnp.zeros((104, TOK), F32)], axis=0)
    cols[...] = stack.T

    def expand(q):
        halves = []
        for i in (0, 2):
            lo = jnp.broadcast_to(cols[:, 8 * q + i : 8 * q + i + 1], (TOK, 128))
            hi = jnp.broadcast_to(cols[:, 8 * q + i + 1 : 8 * q + i + 2], (TOK, 128))
            halves.append(jnp.where(lane128 < 64, lo, hi))
        return jnp.concatenate(halves, axis=1)

    serve(IN, 8)
    serve(GATE, 7)
    use(1, dots_in, 7)
    use(1, dots_in, 8)
    serve_out(2)
    acc_i[...] = acc_i[...].astype(BF16).astype(F32)
    acc_i[0:HALO, :] = acc_i[0:HALO, :] * not_first
    conv = jnp.zeros((TOK, 256), F32)
    for position in range(4):
        conv = conv + acc_i[pl.ds(HALO - 3 + position, TOK), :] * tapi_ref[position : position + 1, :]
    conv = conv * jax.nn.sigmoid(conv)
    xc[...] = conv.astype(BF16)

    head_lane = lax.broadcasted_iota(jnp.int32, (1, 256), 1) // 64
    weighted = (xc[...].astype(F32) * expand(1)).astype(BF16)
    expcum = expand(2)
    decay0 = expcum[255:256]
    decay1 = expcum[511:512]

    serve_out(3)
    got_all(yr.at[0], bct.at[pl.ds(0, 192), :])
    fresh0 = jnp.dot(bct[0:128, 0:256], weighted[0:256], preferred_element_type=F32)
    fresh1 = jnp.dot(bct[0:128, 256:512], weighted[256:512], preferred_element_type=F32)
    end_own = decay1 * fresh0 + fresh1
    total_own = decay0 * decay1
    th, tl = split(jnp.broadcast_to(total_own, (8, 256)))
    tail = jnp.concatenate([th.astype(F32), tl.astype(F32)], axis=0).astype(BF16)
    e_own[0:128, :] = end_own.astype(BF16)
    e_own[128:144, :] = tail
    swap = remote(e_own, e_sib, es.at[0], es.at[1], sib)
    swap.start()

    serve(GATE, 8)
    swap.wait()

    end_sib = e_sib[0:128, :].astype(F32)
    total_sib = e_sib[128:129, :].astype(F32) + e_sib[136:137, :].astype(F32)

    def my_half(value):
        return jnp.where(c == 0, value[:, 0:128], value[:, 128:256])

    second_decay = jnp.where(c == 0, total_sib, total_own)
    chip_end = second_decay * jnp.where(c == 0, end_own, end_sib) + jnp.where(
        c == 0, end_sib, end_own
    )
    chip_total = jnp.broadcast_to(my_half(total_own * total_sib), (8, 128))
    th, tl = split(chip_total)
    tbuf[z, 0:128, :] = my_half(chip_end).astype(BF16)
    tbuf[z, 128:144, :] = jnp.concatenate([th.astype(F32), tl.astype(F32)], axis=0).astype(BF16)

    def t_send(d, k, hop):
        ref = tbuf.at[origin(d, k)]
        target = zmod(z + hop) if d == 0 else zmod(z - hop)
        return remote(ref, ref, ts.at[0], tr.at[d, k + hop - 1], dev(target, c, h))

    def t_recv(d, k):
        ref = tbuf.at[origin(d, k)]
        got_all(tr.at[d, k - 1], ref)

    def t_start(d, k, hop):
        t_send(d, k, hop).start()

    for hop in (2, 1):
        for d in (0, 1):
            t_start(d, 0, hop)

    serve_out(4)

    row = lax.broadcasted_iota(jnp.int32, (256, 256), 0)
    column = lax.broadcasted_iota(jnp.int32, (256, 256), 1)
    c_mat = bct[128:256, :].astype(F32).T.astype(BF16)
    intra = []

    def span(q):
        tokens = slice(256 * q, 256 * q + 256)
        scores = jnp.dot(c_mat[tokens], bct[0:128, tokens], preferred_element_type=F32)
        scores = jnp.where(row >= column, scores, 0.0)
        total = jnp.zeros((256, 256), F32)
        for i in range(4):
            gap = jnp.minimum(cols[tokens, i : i + 1] - cum[i : i + 1, tokens], 0.0)
            mixing = (scores * jnp.exp(gap) * dt[i : i + 1, tokens]).astype(BF16)
            x_head = jnp.where(head_lane == i, xc[tokens, :].astype(F32), 0.0).astype(BF16)
            total = total + jnp.dot(mixing, x_head, preferred_element_type=F32)
        return total

    mixed0 = span(0)

    def gate_half(q):
        tokens = slice(256 * q, 256 * q + 256)
        acc_g[tokens, :] = jnp.dot(
            act[HALO + 256 * q : HALO + 256 * q + 256, :], w_gate[...], preferred_element_type=F32
        )

    got_all(br_gate.at[0], w_gate.at[pl.ds(0, 2048), :])
    gate_half(0)
    for d in (0, 1):
        t_recv(d, 2)
        for hop in (2, 1):
            t_start(d, 2, hop)
    serve_out(5)
    mixed1 = span(1)
    gate_half(1)
    skip = jnp.where(
        head_lane < 2,
        jnp.where(head_lane == 0, skip_ref[0], skip_ref[1]),
        jnp.where(head_lane == 2, skip_ref[2], skip_ref[3]),
    )
    xf = xc[...].astype(F32)
    mixed0 = mixed0 + skip * xf[0:256]
    mixed1 = mixed1 + skip * xf[256:512]
    for d in (0, 1):
        t_recv(d, 4)
        for hop in (2, 1):
            t_start(d, 4, hop)
    serve_out(6)
    t_recv(0, 6)
    for hop in (2, 1):
        t_start(0, 6, hop)
    t_recv(1, 6)
    t_start(1, 6, 1)
    serve_out(7)
    for d, ks in ((0, (1, 3, 5, 7, 8)), (1, (1, 3, 5, 7))):
        for k in ks:
            t_recv(d, k)

    prefix = jnp.zeros((128, 128), F32)
    for k in range(15, 0, -1):
        zz = zmod(z - k)
        decay = tbuf[zz, 128:129, :].astype(F32) + tbuf[zz, 136:137, :].astype(F32)
        joined = decay * prefix + tbuf[zz, 0:128, :].astype(F32)
        prefix = jnp.where(z >= k, joined, prefix)
    pbuf[...] = prefix
    swap2 = remote(pbuf, psib, es.at[2], es.at[3], sib)
    swap2.start()
    serve_out(8)
    swap2.wait()
    other = psib[...]
    before = jnp.where(
        c == 0,
        jnp.concatenate([prefix, other], axis=1),
        jnp.concatenate([other, prefix], axis=1),
    )
    state0 = jnp.where(c == 0, before, total_sib * before + end_sib)
    state1 = decay0 * state0 + fresh0

    def gated(q, mixed, state):
        tokens = slice(256 * q, 256 * q + 256)
        high, low = split(state)
        inter = jnp.dot(c_mat[tokens], high, preferred_element_type=F32)
        inter = inter + jnp.dot(c_mat[tokens], low, preferred_element_type=F32)
        mixed = mixed + inter * expcum[tokens]
        gate = acc_g[tokens, :].astype(BF16).astype(F32)
        gath[tokens, pl.ds(pl.multiple_of(256 * y, 256), 256)] = (
            mixed * (gate * jax.nn.sigmoid(gate))
        ).astype(BF16)

    def part(u, a, first_row, rows):
        column = pl.multiple_of(256 * lax.rem(y + a + 4, 4), 256)
        return gath.at[pl.ds(128 * u + first_row, rows), pl.ds(column, 256)]

    STEP = (1, -1)

    def g_near(u, way, a):
        ref = part(u, a, 0, 128)
        return remote(ref, ref, gs.at[0], gr.at[u, way], dev(z, c, hid_at(0, STEP[way])))

    def g_far(u, way, a):
        ref = part(u, a, 64 * way, 64)
        return remote(
            ref, ref, gs.at[0], gr.at[u, 2], dev(z, c, hid_at(0, STEP[way]))
        )

    def near_start(u):
        for way in (0, 1):
            g_near(u, way, 0).start()

    def near_take(u):
        for way in (0, 1):
            g_near(u, way, -STEP[way]).wait_recv()
            g_far(u, way, -STEP[way]).start()

    gated(0, mixed0, state0)
    near_start(0)
    near_start(1)
    gated(1, mixed1, state1)
    near_start(2)
    serve_out(9)

    def drain_weights():
        sent_all(zs.at[0], w_gs.at[:, pl.ds(0, 1920)])
        sent_all(bs.at[0], w_gs.at[:, pl.ds(0, 2048)])
        for kind, ref in ((1, w_in), (2, w_gate)):
            sent_all(zs.at[kind], ref.at[pl.ds(0, 1920), :])
            sent_all(bs.at[kind], ref.at[pl.ds(0, 2048), :])

    near_take(0)
    near_take(1)
    near_start(3)
    serve_out(10)
    near_take(2)
    serve_out(11)
    near_take(3)
    out_end()

    SPLIT = ((0, 256), (256, 128), (384, 128))

    def product(u, offset):
        start, count = SPLIT[u]
        rows = pl.ds(pl.multiple_of(256 * lax.rem(x + offset, 4), 256), 256)
        return lax.dot_general(
            gath[start : start + count, :],
            w_out[rows, :],
            (((1,), (1,)), ((), ())),
            preferred_element_type=F32,
        )

    def along(u, slot, way, src, dst):
        landed = hr.at[u, way if slot == 0 else 2]
        return remote(src, dst, hs.at[0], landed, dev(z, c, hid_at(STEP[way], 0)))

    def halves(u):
        start, count = SPLIT[u]
        half = count // 2
        return pl.ds(start, half), pl.ds(start + half, half), pl.ds(start // 2, half)

    def far_send(u, way):
        rows = halves(u)
        return along(u, 0, way, s_far.at[rows[way]], (r_up, r_down)[way].at[rows[2]])

    def early_send(u, way):
        rows = halves(u)[1 - way]
        return along(u, 1, way, (s_up, s_down)[way].at[rows], (f_up, f_down)[way].at[rows])

    def late_send(u, way):
        rows = halves(u)[way]
        return along(u, 2, way, (s_up, s_down)[way].at[rows], (f_up, f_down)[way].at[rows])

    def square_send(u, j):
        start, count = SPLIT[u]
        lanes = pl.ds(start, count)
        return remote(
            sq_own.at[:, lanes], sq_in.at[j - 1, :, lanes], qs.at[0], qr.at[u], dev(z, c, hid_at(j, 0))
        )

    def multiply_far(u):
        start, count = SPLIT[u]
        s_far[start : start + count, :] = product(u, 2).astype(BF16)
        for way in (0, 1):
            far_send(u, way).start()

    def multiply_near(u):
        top, low, kept = halves(u)
        half = SPLIT[u][1] // 2
        up = product(u, 1)
        s_up[low, :] = up[half:].astype(BF16)
        early_send(u, 0).start()
        p_up[kept, :] = up[:half]
        down = product(u, 3)
        s_down[top, :] = down[:half].astype(BF16)
        early_send(u, 1).start()
        p_down[kept, :] = down[half:]

    def square(u):
        start, count = SPLIT[u]
        total = jnp.zeros((count, 128), F32)
        for i in range(8):
            g = gath[start : start + count, 128 * i : 128 * i + 128].astype(F32)
            total = total + g * g
        sq_own[:, start : start + count] = jnp.broadcast_to(
            jnp.sum(total.T, axis=0, keepdims=True), (8, count)
        )
        for j in (1, 3, 2):
            square_send(u, j).start()

    def add(u):
        top, low, kept = halves(u)
        far_send(u, 0).wait_recv()
        s_up[top, :] = (p_up[kept, :] + r_up[kept, :].astype(F32)).astype(BF16)
        late_send(u, 0).start()
        far_send(u, 1).wait_recv()
        s_down[low, :] = (p_down[kept, :] + r_down[kept, :].astype(F32)).astype(BF16)
        late_send(u, 1).start()

    def own(u):
        start, count = SPLIT[u]
        p_own[start : start + count, :] = product(u, 0)

    def finish(u):
        start, count = SPLIT[u]
        tokens = slice(start, start + count)
        got_all(qr.at[u], sq_in.at[:, :, pl.ds(start, count)])
        squares = sq_own[:, tokens] + sq_in[0, :, tokens] + sq_in[1, :, tokens] + sq_in[2, :, tokens]
        scale = lax.rsqrt(squares / INNER + 1e-5)
        scale = jnp.broadcast_to(scale[0:1], (128, count)).T
        got_all(hr.at[u, 2], gath.at[pl.ds(0, count // 2), :])
        value = p_own[tokens, :] + f_up[tokens, :].astype(F32) + f_down[tokens, :].astype(F32)
        for half_of in (0, 128):
            out_ref[tokens, half_of : half_of + 128] = (
                value[:, half_of : half_of + 128] * scale
            ).astype(BF16)

    def far_take(u):
        got_all(gr.at[u, 2], part(u, 2, 0, 128))

    far_take(0)
    far_take(1)
    multiply_far(0)
    multiply_near(0)
    far_take(2)
    multiply_far(1)
    multiply_near(1)
    far_take(3)
    multiply_far(2)
    multiply_near(2)
    add(0)
    square(0)
    square(1)
    add(1)
    square(2)
    own(0)
    add(2)
    own(1)
    own(2)
    drain_weights()
    out_drain()
    sent_all(ys.at[0], bct.at[pl.ds(0, 192), :])
    sent_all(ts.at[0], tbuf.at[pl.ds(0, 15)])
    for u in (0, 1, 2):
        finish(u)
    sent_all(gs.at[0], gath.at[pl.ds(0, 384), :])
    sent_all(hs.at[0], gath.at[pl.ds(0, 384), :])
    sent_all(qs.at[0], sq_in)


def local(
    activations,
    w_inner,
    w_gate,
    w_groups,
    w_step,
    w_out,
    conv_inner,
    conv_groups,
    step_bias,
    decay_log,
    skip_gain,
    norm_gain,
):
    anywhere = pl.BlockSpec(memory_space=pl.ANY)
    vmem = pl.BlockSpec(memory_space=pltpu.VMEM)
    dma = pltpu.SemaphoreType.DMA
    return pl.pallas_call(
        kernel,
        out_shape=jax.ShapeDtypeStruct((TOK, 256), BF16),
        in_specs=[anywhere] * 12,
        out_specs=vmem,
        scratch_shapes=[
            pltpu.VMEM((128, 256), BF16),
            pltpu.VMEM((128, 128), BF16),
            pltpu.VMEM((64, 128), BF16),
            pltpu.VMEM((4, 256), F32),
            pltpu.VMEM((4, 128), F32),
            pltpu.SMEM((4,), F32),
            pltpu.SMEM((4,), F32),
            pltpu.SMEM((4,), F32),
            pltpu.VMEM((1, 256), F32),
            dma((9,)),
            pltpu.VMEM((HALO + TOK, 4096), BF16),
            pltpu.VMEM((4096, 256), BF16),
            pltpu.VMEM((4096, 256), BF16),
            pltpu.VMEM((80, 4096), BF16),
            pltpu.VMEM((128, 256), BF16),
            pltpu.VMEM((1024, 1024), BF16),
            pltpu.VMEM((TOK, 1024), BF16),
            pltpu.VMEM((8, TOK), F32),
            pltpu.VMEM((3, 8, TOK), F32),
            pltpu.VMEM((256, 256), F32),
            pltpu.VMEM((256, 256), F32),
            pltpu.VMEM((TOK, 256), F32),
            pltpu.VMEM((TOK, 256), BF16),
            pltpu.VMEM((TOK, 256), BF16),
            pltpu.VMEM((TOK, 256), BF16),
            pltpu.VMEM((256, 256), BF16),
            pltpu.VMEM((256, 256), BF16),
            pltpu.VMEM((TOK, 256), BF16),
            pltpu.VMEM((TOK, 256), BF16),
            pltpu.VMEM((HALO + TOK, 256), F32),
            pltpu.VMEM((TOK, 256), F32),
            pltpu.VMEM((HALO + TOK, 80), F32),
            pltpu.VMEM((256, TOK), BF16),
            pltpu.VMEM((TOK, 256), BF16),
            pltpu.VMEM((TOK, 128), F32),
            pltpu.VMEM((144, 256), BF16),
            pltpu.VMEM((144, 256), BF16),
            pltpu.VMEM((16, 144, 128), BF16),
            pltpu.VMEM((128, 128), F32),
            pltpu.VMEM((128, 128), F32),
            dma((3,)),
            dma((2,)),
            dma((3,)),
            dma((5, 2, 8)),
            dma((3,)),
            dma((2, 2, 9)),
            dma((1,)),
            dma((1,)),
            dma((1,)),
            dma((2,)),
            dma((2, 2, 8)),
            dma((1,)),
            dma((1,)),
            dma((1,)),
            dma((1,)),
            dma((4,)),
            dma((1,)),
            dma((2, 8)),
            dma((1,)),
            dma((4, 3)),
            dma((1,)),
            dma((3,)),
            dma((1,)),
            dma((3, 3)),
        ],
        compiler_params=pltpu.CompilerParams(
            collective_id=0, has_side_effects=True, vmem_limit_bytes=67043328
        ),
    )(
        activations,
        w_inner,
        w_gate,
        w_out,
        w_groups,
        w_step.T,
        conv_inner,
        conv_groups,
        step_bias,
        decay_log,
        skip_gain,
        norm_gain.reshape(1, 256),
    )


def solution(mesh):
    in_specs = (
        P("seq", None),
        P("seq", "hid"),
        P("seq", "hid"),
        P("seq", None),
        P("seq", None),
        P("seq", "hid"),
        P(None, "hid"),
        P(),
        P("hid"),
        P("hid"),
        P("hid"),
        P("hid"),
    )
    return jax.shard_map(
        local, mesh=mesh, in_specs=in_specs, out_specs=P("seq", "hid"), check_vma=False
    )
```

```python
import jax
import jax.numpy as jnp
from jax import lax
from jax.experimental import pallas as pl
from jax.experimental.pallas import tpu as pltpu
from jax.sharding import PartitionSpec as P

F32 = jnp.float32
BF16 = jnp.bfloat16
MESH = pl.DeviceIdType.MESH
INNER = 4096
TOK = 512
HALO = 8
NZ = 16
FAR = ((8, 7), (8, 7), (7, 8), (8, 7), (7, 8))
KIND = (0, 1, 1, 2, 2)


def remote(src, dst, send, recv, device):
    return pltpu.make_async_remote_copy(
        src_ref=src, dst_ref=dst, send_sem=send, recv_sem=recv, device_id=device, device_id_type=MESH
    )


def split(value):
    high = value.astype(BF16)
    return high, (value - high.astype(F32)).astype(BF16)


def kernel(
    act_hbm,
    wi_hbm,
    wg_hbm,
    wo_hbm,
    wgr_hbm,
    wst_hbm,
    tapi_hbm,
    tapg_hbm,
    bias_hbm,
    decay_hbm,
    skip_hbm,
    gain_hbm,
    out_ref,
    wo_ref,
    wgr_ref,
    wst_ref,
    tapi_ref,
    tapg_ref,
    bias_ref,
    decay_ref,
    skip_ref,
    gain_ref,
    small_sem,
    act,
    w_in,
    w_gate,
    w_gs,
    land,
    w_out,
    gath,
    sq_own,
    sq_in,
    p_up,
    p_down,
    p_own,
    s_far,
    s_up,
    s_down,
    r_up,
    r_down,
    f_up,
    f_down,
    acc_i,
    acc_g,
    acc_s,
    bct,
    xc,
    cols,
    e_own,
    e_sib,
    tbuf,
    pbuf,
    psib,
    local_sem,
    halo_sem,
    zs,
    zr,
    bs,
    br,
    br_gate,
    cs,
    cr,
    os_,
    orr,
    ws,
    wr,
    ys,
    yr,
    es,
    ts,
    tr,
    gs,
    gr,
    qs,
    qr,
    hs,
    hr,
):
    s = lax.axis_index("seq")
    h = lax.axis_index("hid")
    z = s // 2
    c = s % 2
    x = h // 4
    y = h % 4

    def dev(zz, cc, hh):
        return {"seq": 2 * zz + cc, "hid": hh}

    def zmod(v):
        return lax.rem(v + 2 * NZ, NZ)

    def hid_at(dx, dy):
        return lax.rem(x + dx + 4, 4) * 4 + lax.rem(y + dy + 4, 4)

    sib = dev(z, 1 - c, h)
    after = {"seq": lax.rem(s + 1, 32), "hid": h}
    extra = {"seq": lax.rem(s + 2 * c - 1 + 32, 32), "hid": h}

    barrier = pltpu.get_barrier_semaphore()
    for step in (1, -1, 2, -2):
        pl.semaphore_signal(barrier, inc=1, device_id=dev(zmod(z + step), c, h), device_id_type=MESH)
    pl.semaphore_signal(barrier, inc=1, device_id=sib, device_id_type=MESH)
    pl.semaphore_signal(barrier, inc=1, device_id=extra, device_id_type=MESH)
    for step in (1, 2, 3):
        for hh in (hid_at(step, 0), hid_at(0, step)):
            pl.semaphore_signal(barrier, inc=1, device_id=dev(z, c, hh), device_id_type=MESH)

    load_act = pltpu.make_async_copy(act_hbm, act.at[pl.ds(HALO, TOK), :], local_sem.at[0])
    own_rows = pl.ds(pl.multiple_of(s * 128, 128), 128)
    load_in = pltpu.make_async_copy(wi_hbm, w_in.at[own_rows, :], local_sem.at[1])
    load_gate = pltpu.make_async_copy(wg_hbm, w_gate.at[own_rows, :], local_sem.at[2])
    group_cols = pl.ds(pl.multiple_of(x * 256 + (y // 2) * 128, 128), 128)
    small = [
        pltpu.make_async_copy(src, dst, small_sem.at[i])
        for i, (src, dst) in enumerate(
            (
                (wgr_hbm.at[:, group_cols], wgr_ref),
                (wst_hbm, wst_ref),
                (wo_hbm, wo_ref),
                (gain_hbm, gain_ref),
                (tapi_hbm, tapi_ref),
                (tapg_hbm.at[:, group_cols], tapg_ref),
                (bias_hbm, bias_ref),
                (decay_hbm, decay_ref),
                (skip_hbm, skip_ref),
            )
        )
    ]
    load_in.start()
    for item in small:
        item.start()
    load_gate.start()
    load_act.start()

    for item in small:
        item.wait()
    tile = wgr_ref[...].astype(F32).T
    half = jnp.where(y % 2 == 0, tile[:64], tile[64:])
    steps_t = wst_ref[...].astype(F32)
    mine = jnp.where(
        x < 2,
        jnp.where(x == 0, steps_t[0:16], steps_t[16:32]),
        jnp.where(x == 2, steps_t[32:48], steps_t[48:64]),
    )
    own_lanes = pl.ds(pl.multiple_of(s * 128, 128), 128)
    w_gs[0:64, own_lanes] = half.astype(BF16)
    w_gs[64:80, own_lanes] = mine.astype(BF16)

    pl.semaphore_wait(barrier, 12)

    send_halo = remote(
        act_hbm.at[pl.ds(TOK - HALO, HALO), :],
        act.at[pl.ds(0, HALO), :],
        halo_sem.at[0],
        halo_sem.at[1],
        after,
    )

    def sent_all(sem, ref):
        remote(ref, ref, sem, sem, sib).wait_send()

    def got_all(sem, ref):
        remote(ref, ref, sem, sem, sib).wait_recv()

    def block(p, zz):
        row = pl.multiple_of((2 * zz + c) * 128, 128)
        if p == 0:
            return w_gs.at[:, pl.ds(row, 128)]
        part = 64 * ((p - 1) % 2)
        if p < 3:
            return w_in.at[pl.ds(row + part, 64), :]
        return w_gate.at[pl.ds(row + part, 64), :]

    def sib_block(kind, zz):
        row = pl.multiple_of((2 * zz + 1 - c) * 128, 128)
        if kind == 0:
            return w_gs.at[:, pl.ds(row, 128)]
        return w_in.at[pl.ds(row, 128), :]

    def origin(d, k):
        return zmod(z - k) if d == 0 else zmod(z + k)

    def ring(p, d, k, recv_k):
        ref = block(p, origin(d, k))
        target = zmod(z + 1) if d == 0 else zmod(z - 1)
        return remote(ref, ref, zs.at[KIND[p]], zr.at[p, d, recv_k - 1], dev(target, c, h))

    def to_sib(p, d, k):
        ref = block(p, origin(d, k))
        kind = KIND[p]
        landed = br_gate.at[0] if kind == 2 else br.at[kind, 0 if k == 8 else d, k]
        return remote(ref, ref, bs.at[kind], landed, sib)

    def from_sib(kind, d, k):
        got_all(br.at[kind, d, k], sib_block(kind, origin(d, k)))

    keeper = z % 4
    is_source = keeper == y

    def out_rows(zz, cc):
        return pl.multiple_of((zz // 4) * 256 + 128 * cc, 128)

    def out_part(a, zz, cc, column):
        return w_out.at[
            pl.ds(out_rows(zz, cc) + 64 * a, 64), pl.ds(pl.multiple_of(256 * column, 256), 256)
        ]

    def bring(column):
        return remote(
            land,
            w_out.at[pl.ds(out_rows(z, c), 128), pl.ds(pl.multiple_of(256 * column, 256), 256)],
            cs.at[0],
            cr.at[0],
            dev(z, c, x * 4 + keeper),
        )

    near = tuple((d + 3) % 4 + 1 for d in (z - y + 16, y - z + 16))
    OUT_FAR = ((8, 7), (7, 8))

    def out_dist(d, q):
        return near[d] + 4 * (q // 4)

    def out_origin(d, q):
        return zmod(z - out_dist(d, q)) if d == 0 else zmod(z + out_dist(d, q))

    def out_send(a, d, zz, column, slot):
        ref = out_part(a, zz, c, column)
        target = zmod(z + 1) if d == 0 else zmod(z - 1)
        return remote(ref, ref, os_.at[d], orr.at[a, d, slot], dev(target, c, h))

    def out_to_sib(a, d, zz, column, slot):
        ref = out_part(a, zz, c, column)
        return remote(ref, ref, ws.at[0], wr.at[0], sib)

    def next_slot(d, q):
        return jnp.where(near[d] < 4, q, q + 4)

    def serve_out(t):
        if t == 0:

            @pl.when(is_source)
            def _():
                got_all(cr.at[0], w_out.at[pl.ds(0, 96), :])

        if t < 4:

            @pl.when(is_source)
            def _():
                for a in (0, 1):
                    for d in (0, 1):
                        out_send(a, d, z, t, t).start()
                    out_to_sib(a, 2, z, t, t).start()

        if t > 0:
            for a in (0, 1):
                for d in (0, 1):
                    q = t - near[d]
                    reach = out_dist(d, q)

                    @pl.when((q >= 0) & (q < 8) & (reach <= OUT_FAR[a][d]))
                    def _():
                        zz, column = out_origin(d, q), q % 4
                        out_send(a, d, zz, column, q).wait_recv()

                        @pl.when(reach < OUT_FAR[a][d])
                        def _():
                            out_send(a, d, zz, column, next_slot(d, q)).start()

                        out_to_sib(a, d, zz, column, q).start()

    def out_end():
        got_all(wr.at[0], w_out.at[pl.ds(0, 512), :])

    def out_drain():
        for d in (0, 1):

            @pl.when(near[d] == 3)
            def _():
                sent_all(os_.at[d], w_out.at[pl.ds(0, 192), :])

            @pl.when(near[d] != 3)
            def _():
                sent_all(os_.at[d], w_out.at[pl.ds(0, 256), :])

        sent_all(ws.at[0], w_out.at[pl.ds(0, 512), :])

        @pl.when(jnp.logical_not(is_source))
        def _():
            sent_all(cs.at[0], land)

    def hand_on(p, d, k):
        to_sib(p, d, k).start()

    def first(p):
        ring(p, 0, 0, 1).start()
        ring(p, 1, 0, 1).start()
        hand_on(p, 0, 0)

    def event(p, d, k, forward):
        ring(p, d, k, k).wait_recv()
        if forward:
            ring(p, d, k, k + 1).start()
        hand_on(p, d, k)

    def columns(zz):
        return pl.ds(pl.multiple_of(zz * 256, 256), 256)

    def dots_in(*planes):
        acc_i[...] += sum(
            jnp.dot(act[:, columns(zz)], w_in[columns(zz), :], preferred_element_type=F32)
            for zz in planes
        )

    def dots_gs(*planes):
        acc_s[...] += sum(
            lax.dot_general(
                act[:, columns(zz)],
                w_gs[:, columns(zz)],
                (((1,), (1,)), ((), ())),
                preferred_element_type=F32,
            )
            for zz in planes
        )

    first(0)
    load_in.wait()
    first(1)
    first(2)
    send_halo.start()
    scaled = (wo_ref[...].astype(F32) * gain_ref[...]).astype(BF16)

    @pl.when(is_source)
    def _():
        w_out[pl.ds(out_rows(z, c), 128), pl.ds(pl.multiple_of(256 * y, 256), 256)] = scaled

    @pl.when(jnp.logical_not(is_source))
    def _():
        land[...] = scaled
        bring(y).start()

    acc_i[...] = jnp.zeros_like(acc_i)
    acc_s[...] = jnp.zeros_like(acc_s)

    def serve(pieces, k):
        for p in pieces:
            for d in (0, 1):
                if k <= FAR[p][d]:
                    event(p, d, k, k < FAR[p][d])

    def use(kind, dots, k):
        from_sib(kind, 0, k)
        if k == 8:
            dots(origin(0, k))
        else:
            from_sib(kind, 1, k)
            dots(origin(0, k), origin(1, k))

    IN = (1, 2)
    GATE = (3, 4)

    serve((0,), 1)
    serve(IN, 1)
    load_gate.wait()
    first(3)
    first(4)
    load_act.wait()
    send_halo.wait()
    for kind in (0, 1):
        from_sib(kind, 0, 0)
    dots_gs(z)
    dots_in(z)
    for k in (2, 3, 4, 5, 6, 7):
        serve((0, 1), k)
        use(0, dots_gs, k - 1)
        serve((2,), k)
        serve((3,), k - 1)
        use(1, dots_in, k - 1)
        serve((4,), k - 1)
    serve_out(0)
    serve((0,), 8)
    use(0, dots_gs, 7)
    use(0, dots_gs, 8)
    serve_out(1)

    not_first = jnp.where(s == 0, 0.0, 1.0).astype(F32)
    lane128 = lax.broadcasted_iota(jnp.int32, (TOK, 128), 1)
    raw = acc_s[HALO:, :]
    acc_s[...] = acc_s[...].astype(BF16).astype(F32)
    acc_s[0:HALO, :] = acc_s[0:HALO, :] * not_first
    tap_tile = tapg_ref[...]
    tap_g = jnp.where(y % 2 == 0, tap_tile, pltpu.roll(tap_tile, 64, axis=1))
    conv = jnp.zeros((TOK, 80), F32)
    for position in range(4):
        conv = conv + acc_s[pl.ds(HALO - 3 + position, TOK), :] * tap_g[position : position + 1, :80]
    conv = conv * jax.nn.sigmoid(conv)
    both = jnp.where(lane128[:, :80] < 64, conv, raw)
    both_t = jnp.concatenate([both, jnp.zeros((TOK, 48), F32)], axis=1).T
    own_cols = pl.ds(pl.multiple_of(64 * y, 64), 64)
    bct[own_cols, :] = both_t[0:64].astype(BF16)

    def y_copy(j, where):
        rows = bct.at[pl.ds(pl.multiple_of(64 * where, 64), 64), :]
        return remote(rows, rows, ys.at[0], yr.at[0], dev(z, c, hid_at(0, j)))

    for j in (1, 3, 2):
        y_copy(j, y).start()

    step4 = jnp.where(
        y < 2,
        jnp.where(y == 0, both_t[64:68], both_t[68:72]),
        jnp.where(y == 2, both_t[72:76], both_t[76:80]),
    )
    step8 = jnp.concatenate([step4, step4], axis=0)
    head = lax.broadcasted_iota(jnp.int32, (8, TOK), 0) % 4
    lane = lax.broadcasted_iota(jnp.int32, (8, TOK), 1)

    def per_head(ref):
        return jnp.where(
            head < 2, jnp.where(head == 0, ref[0], ref[1]), jnp.where(head == 2, ref[2], ref[3])
        )

    v = step8 + per_head(bias_ref)
    dt = jnp.maximum(v, 0.0) + jnp.log1p(jnp.exp(-jnp.abs(v)))
    cum = dt * -jnp.exp(per_head(decay_ref))
    for shift in (1, 2, 4, 8, 16, 32, 64, 128):
        cum = cum + jnp.where(lane % 256 >= shift, pltpu.roll(cum, shift, axis=1), 0.0)
    last = jnp.where(lane < 256, cum[:, 255:256], cum[:, 511:512])
    weight = jnp.exp(last - cum) * dt
    stack = jnp.concatenate([cum, weight, jnp.exp(cum), jnp.zeros((104, TOK), F32)], axis=0)
    cols[...] = stack.T

    def expand(q):
        halves = []
        for i in (0, 2):
            lo = jnp.broadcast_to(cols[:, 8 * q + i : 8 * q + i + 1], (TOK, 128))
            hi = jnp.broadcast_to(cols[:, 8 * q + i + 1 : 8 * q + i + 2], (TOK, 128))
            halves.append(jnp.where(lane128 < 64, lo, hi))
        return jnp.concatenate(halves, axis=1)

    serve(IN, 8)
    serve(GATE, 7)
    use(1, dots_in, 7)
    use(1, dots_in, 8)
    serve_out(2)
    acc_i[...] = acc_i[...].astype(BF16).astype(F32)
    acc_i[0:HALO, :] = acc_i[0:HALO, :] * not_first
    conv = jnp.zeros((TOK, 256), F32)
    for position in range(4):
        conv = conv + acc_i[pl.ds(HALO - 3 + position, TOK), :] * tapi_ref[position : position + 1, :]
    conv = conv * jax.nn.sigmoid(conv)
    xc[...] = conv.astype(BF16)

    head_lane = lax.broadcasted_iota(jnp.int32, (1, 256), 1) // 64
    weighted = (xc[...].astype(F32) * expand(1)).astype(BF16)
    expcum = expand(2)
    decay0 = expcum[255:256]
    decay1 = expcum[511:512]

    serve_out(3)
    got_all(yr.at[0], bct.at[pl.ds(0, 192), :])
    fresh0 = jnp.dot(bct[0:128, 0:256], weighted[0:256], preferred_element_type=F32)
    fresh1 = jnp.dot(bct[0:128, 256:512], weighted[256:512], preferred_element_type=F32)
    end_own = decay1 * fresh0 + fresh1
    total_own = decay0 * decay1
    def decay_rows(value):
        high, low = split(jnp.broadcast_to(value, (8, value.shape[1])))
        first_row = lax.broadcasted_iota(jnp.int32, (8, value.shape[1]), 0) == 0
        return jnp.where(first_row, high.astype(F32), low.astype(F32)).astype(BF16)

    def read_decay(rows):
        rows = rows.astype(F32)
        return rows[0:1] + rows[1:2]

    e_own[0:128, :] = end_own.astype(BF16)
    e_own[128:136, :] = decay_rows(total_own)
    swap = remote(e_own, e_sib, es.at[0], es.at[1], sib)
    swap.start()

    serve(GATE, 8)
    swap.wait()

    end_sib = e_sib[0:128, :].astype(F32)
    total_sib = read_decay(e_sib[128:136, :])

    def my_half(value):
        return jnp.where(c == 0, value[:, 0:128], value[:, 128:256])

    second_decay = jnp.where(c == 0, total_sib, total_own)
    chip_end = second_decay * jnp.where(c == 0, end_own, end_sib) + jnp.where(
        c == 0, end_sib, end_own
    )
    tbuf[z, 0:128, :] = my_half(chip_end).astype(BF16)
    tbuf[z, 128:136, :] = decay_rows(my_half(total_own * total_sib))

    def t_send(d, k, hop):
        ref = tbuf.at[origin(d, k)]
        target = zmod(z + hop) if d == 0 else zmod(z - hop)
        return remote(ref, ref, ts.at[0], tr.at[d, k + hop - 1], dev(target, c, h))

    def t_recv(d, k):
        ref = tbuf.at[origin(d, k)]
        got_all(tr.at[d, k - 1], ref)

    def t_start(d, k, hop):
        t_send(d, k, hop).start()

    for hop in (2, 1):
        for d in (0, 1):
            t_start(d, 0, hop)

    serve_out(4)

    row = lax.broadcasted_iota(jnp.int32, (256, 256), 0)
    column = lax.broadcasted_iota(jnp.int32, (256, 256), 1)
    c_mat = bct[128:256, :].astype(F32).T.astype(BF16)
    intra = []

    def span(q):
        tokens = slice(256 * q, 256 * q + 256)
        scores = jnp.dot(c_mat[tokens], bct[0:128, tokens], preferred_element_type=F32)
        scores = jnp.where(row >= column, scores, 0.0)
        total = jnp.zeros((256, 256), F32)
        for i in range(4):
            gap = jnp.minimum(cols[tokens, i : i + 1] - cum[i : i + 1, tokens], 0.0)
            mixing = (scores * jnp.exp(gap) * dt[i : i + 1, tokens]).astype(BF16)
            x_head = jnp.where(head_lane == i, xc[tokens, :].astype(F32), 0.0).astype(BF16)
            total = total + jnp.dot(mixing, x_head, preferred_element_type=F32)
        return total

    mixed0 = span(0)

    def gate_half(q):
        tokens = slice(256 * q, 256 * q + 256)
        acc_g[tokens, :] = jnp.dot(
            act[HALO + 256 * q : HALO + 256 * q + 256, :], w_gate[...], preferred_element_type=F32
        )

    got_all(br_gate.at[0], w_gate.at[pl.ds(0, 2048), :])
    gate_half(0)
    for d in (0, 1):
        t_recv(d, 2)
        for hop in (2, 1):
            t_start(d, 2, hop)
    serve_out(5)
    mixed1 = span(1)
    gate_half(1)
    skip = jnp.where(
        head_lane < 2,
        jnp.where(head_lane == 0, skip_ref[0], skip_ref[1]),
        jnp.where(head_lane == 2, skip_ref[2], skip_ref[3]),
    )
    xf = xc[...].astype(F32)
    mixed0 = mixed0 + skip * xf[0:256]
    mixed1 = mixed1 + skip * xf[256:512]
    for d in (0, 1):
        t_recv(d, 4)
        for hop in (2, 1):
            t_start(d, 4, hop)
    serve_out(6)
    t_recv(0, 6)
    for hop in (2, 1):
        t_start(0, 6, hop)
    t_recv(1, 6)
    t_start(1, 6, 1)
    serve_out(7)
    for d, ks in ((0, (1, 3, 5, 7, 8)), (1, (1, 3, 5, 7))):
        for k in ks:
            t_recv(d, k)

    prefix = jnp.zeros((128, 128), F32)
    for k in range(15, 0, -1):
        zz = zmod(z - k)
        decay = read_decay(tbuf[zz, 128:136, :])
        joined = decay * prefix + tbuf[zz, 0:128, :].astype(F32)
        prefix = jnp.where(z >= k, joined, prefix)
    pbuf[...] = prefix
    swap2 = remote(pbuf, psib, es.at[2], es.at[3], sib)
    swap2.start()
    serve_out(8)
    swap2.wait()
    other = psib[...]
    before = jnp.where(
        c == 0,
        jnp.concatenate([prefix, other], axis=1),
        jnp.concatenate([other, prefix], axis=1),
    )
    state0 = jnp.where(c == 0, before, total_sib * before + end_sib)
    state1 = decay0 * state0 + fresh0

    def gated(q, mixed, state):
        tokens = slice(256 * q, 256 * q + 256)
        high, low = split(state)
        inter = jnp.dot(c_mat[tokens], high, preferred_element_type=F32)
        inter = inter + jnp.dot(c_mat[tokens], low, preferred_element_type=F32)
        mixed = mixed + inter * expcum[tokens]
        gate = acc_g[tokens, :].astype(BF16).astype(F32)
        gath[tokens, pl.ds(pl.multiple_of(256 * y, 256), 256)] = (
            mixed * (gate * jax.nn.sigmoid(gate))
        ).astype(BF16)

    def part(u, a, first_row, rows):
        column = pl.multiple_of(256 * lax.rem(y + a + 4, 4), 256)
        return gath.at[pl.ds(128 * u + first_row, rows), pl.ds(column, 256)]

    STEP = (1, -1)

    def g_near(u, way, a):
        ref = part(u, a, 0, 128)
        return remote(ref, ref, gs.at[0], gr.at[u, way], dev(z, c, hid_at(0, STEP[way])))

    def g_far(u, way, a):
        ref = part(u, a, 64 * way, 64)
        return remote(
            ref, ref, gs.at[0], gr.at[u, 2], dev(z, c, hid_at(0, STEP[way]))
        )

    def near_start(u):
        for way in (0, 1):
            g_near(u, way, 0).start()

    def near_take(u):
        for way in (0, 1):
            g_near(u, way, -STEP[way]).wait_recv()
            g_far(u, way, -STEP[way]).start()

    gated(0, mixed0, state0)
    near_start(0)
    near_start(1)
    gated(1, mixed1, state1)
    near_start(2)
    serve_out(9)

    def drain_weights():
        sent_all(zs.at[0], w_gs.at[:, pl.ds(0, 1920)])
        sent_all(bs.at[0], w_gs.at[:, pl.ds(0, 2048)])
        for kind, ref in ((1, w_in), (2, w_gate)):
            sent_all(zs.at[kind], ref.at[pl.ds(0, 1920), :])
            sent_all(bs.at[kind], ref.at[pl.ds(0, 2048), :])

    near_take(0)
    near_take(1)
    near_start(3)
    serve_out(10)
    near_take(2)
    serve_out(11)
    near_take(3)
    out_end()

    SPLIT = ((0, 256), (256, 128), (384, 128))

    def product(u, offset):
        start, count = SPLIT[u]
        rows = pl.ds(pl.multiple_of(256 * lax.rem(x + offset, 4), 256), 256)
        return lax.dot_general(
            gath[start : start + count, :],
            w_out[rows, :],
            (((1,), (1,)), ((), ())),
            preferred_element_type=F32,
        )

    def along(u, slot, way, src, dst):
        landed = hr.at[u, way if slot == 0 else 2]
        return remote(src, dst, hs.at[0], landed, dev(z, c, hid_at(STEP[way], 0)))

    def halves(u):
        start, count = SPLIT[u]
        half = count // 2
        return pl.ds(start, half), pl.ds(start + half, half), pl.ds(start // 2, half)

    def far_send(u, way):
        rows = halves(u)
        return along(u, 0, way, s_far.at[rows[way]], (r_up, r_down)[way].at[rows[2]])

    def early_send(u, way):
        rows = halves(u)[1 - way]
        return along(u, 1, way, (s_up, s_down)[way].at[rows], (f_up, f_down)[way].at[rows])

    def late_send(u, way):
        rows = halves(u)[way]
        return along(u, 2, way, (s_up, s_down)[way].at[rows], (f_up, f_down)[way].at[rows])

    def square_send(u, j):
        start, count = SPLIT[u]
        lanes = pl.ds(start, count)
        return remote(
            sq_own.at[:, lanes], sq_in.at[j - 1, :, lanes], qs.at[0], qr.at[u], dev(z, c, hid_at(j, 0))
        )

    def multiply_far(u):
        start, count = SPLIT[u]
        s_far[start : start + count, :] = product(u, 2).astype(BF16)
        for way in (0, 1):
            far_send(u, way).start()

    def multiply_near(u):
        top, low, kept = halves(u)
        half = SPLIT[u][1] // 2
        up = product(u, 1)
        s_up[low, :] = up[half:].astype(BF16)
        early_send(u, 0).start()
        p_up[kept, :] = up[:half]
        down = product(u, 3)
        s_down[top, :] = down[:half].astype(BF16)
        early_send(u, 1).start()
        p_down[kept, :] = down[half:]

    def square(u):
        start, count = SPLIT[u]
        total = jnp.zeros((count, 128), F32)
        for i in range(8):
            g = gath[start : start + count, 128 * i : 128 * i + 128].astype(F32)
            total = total + g * g
        sq_own[:, start : start + count] = jnp.broadcast_to(
            jnp.sum(total.T, axis=0, keepdims=True), (8, count)
        )
        for j in (1, 3, 2):
            square_send(u, j).start()

    def add(u):
        top, low, kept = halves(u)
        far_send(u, 0).wait_recv()
        s_up[top, :] = (p_up[kept, :] + r_up[kept, :].astype(F32)).astype(BF16)
        late_send(u, 0).start()
        far_send(u, 1).wait_recv()
        s_down[low, :] = (p_down[kept, :] + r_down[kept, :].astype(F32)).astype(BF16)
        late_send(u, 1).start()

    def own(u):
        start, count = SPLIT[u]
        p_own[start : start + count, :] = product(u, 0)

    def finish(u):
        start, count = SPLIT[u]
        tokens = slice(start, start + count)
        got_all(qr.at[u], sq_in.at[:, :, pl.ds(start, count)])
        squares = sq_own[:, tokens] + sq_in[0, :, tokens] + sq_in[1, :, tokens] + sq_in[2, :, tokens]
        scale = lax.rsqrt(squares / INNER + 1e-5)
        scale = jnp.broadcast_to(scale[0:1], (128, count)).T
        got_all(hr.at[u, 2], gath.at[pl.ds(0, count // 2), :])
        value = p_own[tokens, :] + f_up[tokens, :].astype(F32) + f_down[tokens, :].astype(F32)
        for half_of in (0, 128):
            out_ref[tokens, half_of : half_of + 128] = (
                value[:, half_of : half_of + 128] * scale
            ).astype(BF16)

    def far_take(u):
        got_all(gr.at[u, 2], part(u, 2, 0, 128))

    far_take(0)
    far_take(1)
    multiply_far(0)
    multiply_near(0)
    far_take(2)
    multiply_far(1)
    multiply_near(1)
    far_take(3)
    multiply_far(2)
    multiply_near(2)
    add(0)
    square(0)
    square(1)
    add(1)
    square(2)
    own(0)
    add(2)
    own(1)
    own(2)
    drain_weights()
    out_drain()
    sent_all(ys.at[0], bct.at[pl.ds(0, 192), :])
    sent_all(ts.at[0], tbuf.at[pl.ds(0, 15)])
    for u in (0, 1, 2):
        finish(u)
    sent_all(gs.at[0], gath.at[pl.ds(0, 384), :])
    sent_all(hs.at[0], gath.at[pl.ds(0, 384), :])
    sent_all(qs.at[0], sq_in)


def local(
    activations,
    w_inner,
    w_gate,
    w_groups,
    w_step,
    w_out,
    conv_inner,
    conv_groups,
    step_bias,
    decay_log,
    skip_gain,
    norm_gain,
):
    anywhere = pl.BlockSpec(memory_space=pl.ANY)
    vmem = pl.BlockSpec(memory_space=pltpu.VMEM)
    dma = pltpu.SemaphoreType.DMA
    return pl.pallas_call(
        kernel,
        out_shape=jax.ShapeDtypeStruct((TOK, 256), BF16),
        in_specs=[anywhere] * 12,
        out_specs=vmem,
        scratch_shapes=[
            pltpu.VMEM((128, 256), BF16),
            pltpu.VMEM((128, 128), BF16),
            pltpu.VMEM((64, 128), BF16),
            pltpu.VMEM((4, 256), F32),
            pltpu.VMEM((4, 128), F32),
            pltpu.SMEM((4,), F32),
            pltpu.SMEM((4,), F32),
            pltpu.SMEM((4,), F32),
            pltpu.VMEM((1, 256), F32),
            dma((9,)),
            pltpu.VMEM((HALO + TOK, 4096), BF16),
            pltpu.VMEM((4096, 256), BF16),
            pltpu.VMEM((4096, 256), BF16),
            pltpu.VMEM((80, 4096), BF16),
            pltpu.VMEM((128, 256), BF16),
            pltpu.VMEM((1024, 1024), BF16),
            pltpu.VMEM((TOK, 1024), BF16),
            pltpu.VMEM((8, TOK), F32),
            pltpu.VMEM((3, 8, TOK), F32),
            pltpu.VMEM((256, 256), F32),
            pltpu.VMEM((256, 256), F32),
            pltpu.VMEM((TOK, 256), F32),
            pltpu.VMEM((TOK, 256), BF16),
            pltpu.VMEM((TOK, 256), BF16),
            pltpu.VMEM((TOK, 256), BF16),
            pltpu.VMEM((256, 256), BF16),
            pltpu.VMEM((256, 256), BF16),
            pltpu.VMEM((TOK, 256), BF16),
            pltpu.VMEM((TOK, 256), BF16),
            pltpu.VMEM((HALO + TOK, 256), F32),
            pltpu.VMEM((TOK, 256), F32),
            pltpu.VMEM((HALO + TOK, 80), F32),
            pltpu.VMEM((256, TOK), BF16),
            pltpu.VMEM((TOK, 256), BF16),
            pltpu.VMEM((TOK, 128), F32),
            pltpu.VMEM((136, 256), BF16),
            pltpu.VMEM((136, 256), BF16),
            pltpu.VMEM((16, 136, 128), BF16),
            pltpu.VMEM((128, 128), F32),
            pltpu.VMEM((128, 128), F32),
            dma((3,)),
            dma((2,)),
            dma((3,)),
            dma((5, 2, 8)),
            dma((3,)),
            dma((2, 2, 9)),
            dma((1,)),
            dma((1,)),
            dma((1,)),
            dma((2,)),
            dma((2, 2, 8)),
            dma((1,)),
            dma((1,)),
            dma((1,)),
            dma((1,)),
            dma((4,)),
            dma((1,)),
            dma((2, 8)),
            dma((1,)),
            dma((4, 3)),
            dma((1,)),
            dma((3,)),
            dma((1,)),
            dma((3, 3)),
        ],
        compiler_params=pltpu.CompilerParams(
            collective_id=0, has_side_effects=True, vmem_limit_bytes=67043328
        ),
    )(
        activations,
        w_inner,
        w_gate,
        w_out,
        w_groups,
        w_step.T,
        conv_inner,
        conv_groups,
        step_bias,
        decay_log,
        skip_gain,
        norm_gain.reshape(1, 256),
    )


def solution(mesh):
    in_specs = (
        P("seq", None),
        P("seq", "hid"),
        P("seq", "hid"),
        P("seq", None),
        P("seq", None),
        P("seq", "hid"),
        P(None, "hid"),
        P(),
        P("hid"),
        P("hid"),
        P("hid"),
        P("hid"),
    )
    return jax.shard_map(
        local, mesh=mesh, in_specs=in_specs, out_specs=P("seq", "hid"), check_vma=False
    )
```
